32 devices in a mesh: wide: 4 (over z), narrow: 8 (over y, x, core).
Axes of the slice: x: 2, y: 2, z: 4, core: 2. Of those that a mesh axis runs over, the one named last changes fastest.
Arguments:
- acts: bfloat16 [32, 128, 2048], P(('wide', 'narrow')), parts along dimension 0, may hold values from -6 to 6
- cotangent: bfloat16 [32, 128, 2048], P(('wide', 'narrow')), parts along dimension 0, may hold values from -0.5 to 0.5
- down_matrix: bfloat16 [64, 2048], replicated, may hold values from -0.125 to 0.125
- up_matrix: bfloat16 [2048, 64], replicated, may hold values from -0.125 to 0.125
- adam_first_moment: float32 [262144], P('narrow'), may hold values from -0.6 to 0.6
- adam_second_moment: float32 [262144], P('narrow'), may hold values from 0.05 to 5
- lengths: int32 [32], P(('wide', 'narrow')), parts along dimension 0, may hold values from 32 to 128, as said below
- sign_hash_salt: int32 [1], replicated, may hold values from 0 to 999999
Outputs:
- features: float32 [32, 4096], P(('wide', 'narrow')), parts along dimension 0
The draws below stay inside these ranges and needn't reach their ends.
There are 4 independent parts, one for each index of `wide`. The reference program is written for one: setup_inputs(seed, part) draws one part's arguments, and reference() takes and returns one part's arrays. A program takes and returns all parts, laid end to end along the dimension named above; an argument that names none is the same for every part. Nothing has to cross between parts.
Inputs may be any that keep to these rules, and one draw needn't show every extreme that they name: `lengths`: tokens at or after a sequence's length are padding. Some sequence of each batch has exactly 128 and another exactly 32.
All inputs are finite; a program needn't handle non-finite values.
Results may differ from the reference program's by a relative error of at most 0.0033.
Values may be sent and summed in bfloat16 or wider, within the bound.
No kernel may reach another device: no remote copies, remote signals or barrier semaphores. Data moves between devices by JAX's collectives and lax.ppermute only.
A program may use at most 64 MiB of HBM per device.

```python
import math
import jax
import jax.numpy as jnp
from jax import lax

INPUT_DIM = 2048
ADAPTER_RANK = 64
FEAT = 4096
LEN = 128
PARAMS = 262144
SEQ = 8


def draw_lengths(key, part):
    key_lens = jax.random.fold_in(key, 11)
    key_full = jax.random.fold_in(key, 12)
    key_short = jax.random.fold_in(key, 13)
    lens = jax.random.randint(key_lens, (SEQ,), LEN // 4, LEN + 1, dtype=jnp.int32)
    longest = jax.random.randint(key_full, (), 0, SEQ, dtype=jnp.int32)
    offset = jax.random.randint(key_short, (), 1, SEQ, dtype=jnp.int32)
    shortest = (longest + offset) % SEQ
    lens = lens.at[longest].set(LEN)
    lens = lens.at[shortest].set(LEN // 4)
    return lens


def block_scale(stream_key, extent, cuts, low, largest):
    factor_of, own = 1.0, jax.random.fold_in(stream_key, 6)
    for axis_at, shards_of in cuts:
        draws = jnp.exp(jax.random.uniform(jax.random.fold_in(own, axis_at), (shards_of,), jnp.float32, low / len(cuts), largest / len(cuts)))
        factor_of = factor_of * jnp.repeat(draws, extent[axis_at] // shards_of).reshape([-1 if axis == axis_at else 1 for axis in range(len(extent))])
    return factor_of


def bell_draw(own_key, extent, scale, limit, cuts=(), kind=jnp.bfloat16):
    result = jax.random.normal(own_key, extent, jnp.float32) * scale
    if len(cuts) > 0:
        result = block_scale(own_key, extent, cuts, -0.22, 0.18) * result
    return jnp.clip(result, min=-limit, max=limit).astype(kind)


def setup_inputs(seed: int = 0, part: int = 0) -> dict:
    arg_keys = jax.random.split(jax.random.key(seed), 9)
    part_keys = jax.random.split(jax.random.fold_in(arg_keys[8], part), 9)
    return {
        "acts": bell_draw(part_keys[0], (SEQ, LEN, INPUT_DIM), 1.0, 6.0, ((0, 8),)),
        "cotangent": bell_draw(part_keys[1], (SEQ, LEN, INPUT_DIM), 0.0625, 0.5, ((0, 8),)),
        "down_matrix": bell_draw(arg_keys[2], (ADAPTER_RANK, INPUT_DIM), INPUT_DIM ** -0.5, 0.125),
        "up_matrix": bell_draw(arg_keys[3], (INPUT_DIM, ADAPTER_RANK), INPUT_DIM ** -0.5, 0.125),
        "adam_first_moment": bell_draw(arg_keys[4], (PARAMS,), 0.1, 0.6, ((0, 8),), jnp.float32),
        "adam_second_moment": jnp.clip(jnp.exp(math.log(5.0) - 4.6051702 * jax.random.uniform(arg_keys[5], (PARAMS,), jnp.float32) ** block_scale(arg_keys[5], (PARAMS,), ((0, 8),), -0.2, 0.2)), 0.05, 5.0),
        "lengths": draw_lengths(jax.random.fold_in(jax.random.fold_in(arg_keys[8], part), 71), part),
        "sign_hash_salt": jax.random.randint(arg_keys[7], (1,), 0, 1000000).astype(jnp.int32),
    }


def rademacher(row_start, rows, col_start, cols, sign_hash_salt):
    row = lax.broadcasted_iota(jnp.int32, (rows, cols), 0) + row_start
    col = lax.broadcasted_iota(jnp.int32, (rows, cols), 1) + col_start
    mixed = row * FEAT + col ^ sign_hash_salt[0]
    mixed = mixed * 747796405 + 1
    mixed = mixed ^ mixed >> 15
    mixed = mixed * 277803737
    mixed = mixed ^ mixed >> 13
    return (1 - 2 * (mixed >> 7 & 1)).astype(jnp.bfloat16)

def reference(acts, cotangent, down_matrix, up_matrix, adam_first_moment, adam_second_moment, lengths, sign_hash_salt):
    positions = jnp.arange(LEN, dtype=jnp.int32)
    mask = (positions[None, :] < lengths[:, None]).astype(jnp.bfloat16)
    masked_tokens = cotangent * mask[:, :, None]
    activation_floats = acts.astype(jnp.float32)
    masked_floats = masked_tokens.astype(jnp.float32)
    hidden_state = jnp.einsum('tyn,jn->tyj', activation_floats, down_matrix.astype(jnp.float32)).astype(jnp.bfloat16)
    inner_product = jnp.einsum('ofy,yj->ofj', masked_floats, up_matrix.astype(jnp.float32)).astype(jnp.bfloat16)
    down_gradient = jnp.einsum('uwj,uwi->uji', inner_product.astype(jnp.float32), activation_floats)
    up_gradient = jnp.einsum('uwj,uwi->uji', hidden_state.astype(jnp.float32), masked_floats)
    grads = jnp.concatenate([down_gradient, up_gradient], axis=1).reshape(acts.shape[0], PARAMS)
    moment_one = 0.9 * adam_first_moment[None, :] + 0.1 * grads
    moment_two = 0.999 * adam_second_moment[None, :] + 0.001 * grads * grads
    updates = (moment_one / (jnp.sqrt(moment_two) + 1e-08)).astype(jnp.bfloat16)
    block = math.gcd(PARAMS, 2048)
    count = PARAMS // block

    def step(total, index):
        start = index * block
        rows = lax.dynamic_slice_in_dim(updates, start, block, 1)
        signs = rademacher(start, block, 0, FEAT, sign_hash_salt)
        return (total + jnp.dot(rows, signs, preferred_element_type=jnp.float32), None)
    total, _ = lax.scan(step, jnp.zeros((acts.shape[0], FEAT), jnp.float32), jnp.arange(count, dtype=jnp.int32))
    return total * PARAMS ** (-0.5)
```

```python
import functools
import math

import jax
import jax.numpy as jnp
import numpy as np
from jax import lax
from jax.experimental import pallas as pl
from jax.experimental.pallas import tpu as pltpu
from jax.sharding import PartitionSpec as P

FEAT = 4096
MUL_A = 747796405
MUL_B = 277803737
AXES = ("wide", "narrow")
COLUMN_BITS = 11
LOW = (1 << COLUMN_BITS) - 1
TILE = 256
I16 = jnp.int16
I32 = jnp.int32


def short(value):
    value &= 0xFFFF
    return np.int16(value - 65536 if value >= 32768 else value)


def grads_kernel(length_ref, acts_ref, cot_ref, down_ref, up_ref, grads_ref):
    rank = down_ref.shape[0]
    acts = acts_ref[...]
    slots = lax.broadcasted_iota(I32, cot_ref.shape, 0)
    masked = jnp.where(slots < length_ref[0], cot_ref[...].astype(jnp.float32), 0.0)
    masked = masked.astype(jnp.bfloat16)
    last = (((1,), (1,)), ((), ()))
    first = (((0,), (0,)), ((), ()))
    hidden = lax.dot_general(acts, down_ref[...], last, preferred_element_type=jnp.float32)
    inner = jnp.dot(masked, up_ref[...], preferred_element_type=jnp.float32)
    grads_ref[:rank, :] = lax.dot_general(
        inner.astype(jnp.bfloat16), acts, first, preferred_element_type=jnp.float32
    )
    grads_ref[rank:, :] = lax.dot_general(
        hidden.astype(jnp.bfloat16), masked, first, preferred_element_type=jnp.float32
    )


def sequence_grads(acts, cotangent, down_matrix, up_matrix, lengths):
    rank, inputs = down_matrix.shape
    vmem = pl.BlockSpec(memory_space=pltpu.VMEM)
    return pl.pallas_call(
        grads_kernel,
        out_shape=jax.ShapeDtypeStruct((2 * rank, inputs), jnp.float32),
        in_specs=[pl.BlockSpec(memory_space=pltpu.SMEM)] + [vmem] * 4,
        out_specs=vmem,
        name="grads",
    )(lengths, acts[0], cotangent[0], down_matrix, up_matrix)


def lane_terms(info_ref, tile):
    salt = info_ref[0]
    feature = lax.broadcasted_iota(I32, (8, TILE), 1) + tile * TILE
    product = (feature ^ (salt & (FEAT - 1))) * MUL_A + 1
    low = product & (FEAT - 1)
    high = lax.shift_right_logical(product, 12)

    def packed(x):
        return jnp.concatenate([x, x], 0).astype(I16)

    return (
        packed(high & LOW),
        packed(((high >> COLUMN_BITS) & 511) + 256),
        packed(low >> 8),
        packed((low & 255) << 3),
    )


def column_terms(info_ref, lanes, block):
    lane_low, lane_high, lane_top, lane_byte = lanes
    salt_row = info_ref[0] >> 12
    column = lax.broadcasted_iota(I32, (16, 128), 0) + (info_ref[2] + block * 16)
    product = ((column ^ (salt_row & LOW)) * MUL_A) & 0xFFFFF
    row_low = (product & LOW).astype(I16)
    row_high = (product >> COLUMN_BITS).astype(I16)
    wide = (1, TILE // 128)
    row_low, row_high = jnp.tile(row_low, wide), jnp.tile(row_high, wide)
    total = row_low + lane_low
    height = row_high + lane_high + lax.shift_right_logical(total, I16(COLUMN_BITS))
    mixed = total * I16(16) + lane_top
    byte8 = (total ^ lane_byte) & I16(0x7F8)
    byte = lax.shift_right_logical(byte8, I16(3))
    tail = byte * I16(MUL_B & 255)
    carry = byte8 * short(MUL_B >> 8) + lax.shift_right_logical(tail, I16(5))
    carry = carry + ((tail * I16(256)) & I16(-32768))
    return height, mixed, carry


def row_heights(info_ref, rows):
    return [
        (((info_ref[1] + k) ^ (info_ref[0] >> (12 + COLUMN_BITS))) * MUL_A) & 511
        for k in range(rows)
    ]


def regroup(updates_ref, grouped_ref, rows, columns):
    lane = lax.broadcasted_iota(I32, (updates_ref.shape[0], 128), 1)
    for half in range(rows // 8):
        for part in range(columns // 128):
            pieces = [
                updates_ref[:, pl.ds((half * 8 + k) * columns + part * 128, 128)]
                for k in range(8)
            ]
            for step in (4, 2, 1):
                upper = ((lane // 16) & step) != 0
                for k in range(8):
                    if k & step:
                        continue
                    a, b = pieces[k], pieces[k + step]
                    pieces[k] = jnp.where(upper, pltpu.roll(b, 16 * step, 1), a)
                    pieces[k + step] = jnp.where(upper, b, pltpu.roll(a, 128 - 16 * step, 1))
            for c in range(8):
                grouped_ref[part * 8 + c, :, half * 128 : half * 128 + 128] = pieces[c].astype(
                    jnp.bfloat16
                )


def project_kernel(rows, columns, info_ref, updates_ref, out_ref, grouped_ref):
    tile = pl.program_id(0)

    @pl.when(tile == 0)
    def _():
        if columns:
            regroup(updates_ref, grouped_ref, rows, columns)
        else:
            grouped_ref[...] = updates_ref[...].astype(jnp.bfloat16)

    lanes = lane_terms(info_ref, tile)
    heights = row_heights(info_ref, rows)
    heights = [jnp.full((16, TILE), h, I32).astype(I16) for h in heights]

    def add_block(block, total):
        height, mixed, carry = column_terms(info_ref, lanes, block)
        signs = []
        for k in range(rows):
            value = (((height + heights[k]) & I16(511)) - I16(256)) ^ mixed
            value = value * short(8 * MUL_B) + carry
            signs.append(jnp.where(value < 0, jnp.bfloat16(-1), jnp.bfloat16(1)))
        signs = jnp.concatenate(signs, 0)
        return total + jnp.dot(grouped_ref[block], signs, preferred_element_type=jnp.float32)

    out_ref[...] = lax.fori_loop(
        0, grouped_ref.shape[0], add_block, jnp.zeros(out_ref.shape, jnp.float32)
    )


def project(info, updates):
    m, rows, columns = updates.shape
    blocks = columns // 16
    if rows % 8 == 0 and columns % 128 == 0:
        flat = updates.reshape(m, rows * columns)
        inside = columns
    else:
        flat = updates.reshape(m, rows, blocks, 16).transpose(2, 0, 1, 3)
        flat = flat.reshape(blocks, m, rows * 16)
        inside = 0
    whole = pl.BlockSpec(flat.shape, lambda t, i: (0,) * flat.ndim)
    return pl.pallas_call(
        functools.partial(project_kernel, rows, inside),
        out_shape=jax.ShapeDtypeStruct((m, FEAT), jnp.float32),
        grid_spec=pltpu.PrefetchScalarGridSpec(
            num_scalar_prefetch=1,
            grid=(FEAT // TILE,),
            in_specs=[whole],
            out_specs=pl.BlockSpec((m, TILE), lambda t, i: (0, t)),
            scratch_shapes=[pltpu.VMEM((blocks, m, rows * 16), jnp.bfloat16)],
        ),
        name="project",
    )(info, flat)


def body(
    groups,
    holders,
    acts,
    cotangent,
    down_matrix,
    up_matrix,
    adam_first_moment,
    adam_second_moment,
    lengths,
    sign_hash_salt,
):
    rank, inputs = down_matrix.shape
    rank_rows = 2 * rank
    rows, columns = rank_rows // holders, inputs // groups
    devices = groups * holders
    params = rank_rows * inputs
    bound = acts.shape[1] * inputs * 6 * 0.125 * 0.5
    scale = 2.0 ** -max(0, math.ceil(math.log2(bound / 60000)))
    group, holder = lax.axis_index("wide"), lax.axis_index("narrow")

    grads = sequence_grads(acts, cotangent, down_matrix, up_matrix, lengths)
    sent = (grads * scale).astype(jnp.float16).reshape(holders, rows, groups, columns)
    sent = sent.transpose(2, 0, 1, 3).reshape(devices, rows, columns)
    grads = lax.all_to_all(sent, AXES, 0, 0, tiled=True).astype(jnp.float32) * (1 / scale)

    def share(moment):
        return lax.dynamic_slice_in_dim(moment.reshape(rows, inputs), group * columns, columns, 1)

    first, second = share(adam_first_moment), share(adam_second_moment)
    moment_one = 0.9 * first[None] + 0.1 * grads
    moment_two = 0.999 * second[None] + 0.001 * grads * grads
    updates = (moment_one / (jnp.sqrt(moment_two) + 1e-08)).astype(jnp.bfloat16)

    info = jnp.stack([sign_hash_salt[0], holder * rows, group * columns])
    partial = project(info, updates) * params**-0.5
    parts = lax.all_to_all(partial.astype(jnp.float16), AXES, 0, 0, tiled=True)
    return jnp.sum(parts.astype(jnp.float32), axis=0, keepdims=True)


def solution(mesh):
    groups, holders = mesh.shape["wide"], mesh.shape["narrow"]
    placed = (
        P(AXES, None, None),
        P(AXES, None, None),
        P(),
        P(),
        P("narrow"),
        P("narrow"),
        P(AXES),
        P(),
    )
    return jax.shard_map(
        functools.partial(body, groups, holders),
        mesh=mesh,
        in_specs=placed,
        out_specs=P(AXES, None),
        check_vma=False,
    )
```

```python
import functools
import math

import jax
import jax.numpy as jnp
import numpy as np
from jax import lax
from jax.experimental import pallas as pl
from jax.experimental.pallas import tpu as pltpu
from jax.sharding import PartitionSpec as P

FEAT = 4096
MUL_A = 747796405
MUL_B = 277803737
AXES = ("wide", "narrow")
COLUMN_BITS = 11
LOW = (1 << COLUMN_BITS) - 1
TILE = 512
GROUP = 32
I16 = jnp.int16
I32 = jnp.int32


def short(value):
    value &= 0xFFFF
    return np.int16(value - 65536 if value >= 32768 else value)


def grads_kernel(holders, length_ref, acts_ref, cot_ref, down_ref, up_ref, grads_ref):
    groups, (rows, columns) = grads_ref.shape[0] // holders, grads_ref.shape[1:]
    acts = acts_ref[...]
    slots = lax.broadcasted_iota(I32, cot_ref.shape, 0)
    masked = jnp.where(slots < length_ref[0], cot_ref[...].astype(jnp.float32), 0.0)
    masked = masked.astype(jnp.bfloat16)
    last = (((1,), (1,)), ((), ()))
    first = (((0,), (0,)), ((), ()))
    hidden = lax.dot_general(acts, down_ref[...], last, preferred_element_type=jnp.float32)
    inner = lax.dot_general(masked, up_ref[...], last, preferred_element_type=jnp.float32)
    for half, (left, right) in enumerate(((inner, acts), (hidden, masked))):
        grads = lax.dot_general(
            left.astype(jnp.bfloat16), right, first, preferred_element_type=jnp.float32
        )
        for holder in range(holders // 2):
            for group in range(groups):
                grads_ref[group * holders + half * (holders // 2) + holder] = grads[
                    holder * rows : (holder + 1) * rows, group * columns : (group + 1) * columns
                ]


def sequence_grads(groups, holders, acts, cotangent, down_matrix, up_matrix, lengths):
    rank, inputs = down_matrix.shape
    vmem = pl.BlockSpec(memory_space=pltpu.VMEM)
    slabs = (groups * holders, 2 * rank // holders, inputs // groups)
    return pl.pallas_call(
        functools.partial(grads_kernel, holders),
        out_shape=jax.ShapeDtypeStruct(slabs, jnp.float32),
        in_specs=[pl.BlockSpec(memory_space=pltpu.SMEM)] + [vmem] * 4,
        out_specs=vmem,
        name="grads",
    )(lengths, acts[0], cotangent[0], down_matrix, up_matrix.T)


def lane_terms(info_ref, tile):
    salt = info_ref[0]
    feature = lax.broadcasted_iota(I32, (8, TILE), 1) + tile * TILE
    product = (feature ^ (salt & (FEAT - 1))) * MUL_A + 1
    low = product & (FEAT - 1)
    high = lax.shift_right_logical(product, 12)

    def packed(x):
        return jnp.concatenate([x, x], 0).astype(I16)

    return (
        packed(high & LOW),
        packed(((high >> COLUMN_BITS) & 511) + 256),
        packed(low >> 8),
        packed((low & 255) << 3),
    )


def column_terms(info_ref, lanes, block):
    lane_low, lane_high, lane_top, lane_byte = lanes
    salt_row = info_ref[0] >> 12
    column = lax.broadcasted_iota(I32, (16, 128), 0) + (info_ref[2] + block * 16)
    product = ((column ^ (salt_row & LOW)) * MUL_A) & 0xFFFFF
    row_low = (product & LOW).astype(I16)
    row_high = (product >> COLUMN_BITS).astype(I16)
    wide = (1, TILE // 128)
    row_low, row_high = jnp.tile(row_low, wide), jnp.tile(row_high, wide)
    total = row_low + lane_low
    height = row_high + lane_high + lax.shift_right_logical(total, I16(COLUMN_BITS))
    mixed = total * I16(16) + lane_top
    byte8 = (total ^ lane_byte) & I16(0x7F8)
    byte = lax.shift_right_logical(byte8, I16(3))
    tail = byte * I16(MUL_B & 255)
    carry = byte8 * short(MUL_B >> 8) + lax.shift_right_logical(tail, I16(5))
    carry = carry + ((tail * I16(256)) & I16(-32768))
    return height, mixed, carry


def row_heights(info_ref, rows):
    return [
        (((info_ref[1] + k) ^ (info_ref[0] >> (12 + COLUMN_BITS))) * MUL_A) & 511
        for k in range(rows)
    ]


def regroup(updates_ref, grouped_ref, staged_ref, rows, columns):
    devices = grouped_ref.shape[1]
    lane = lax.broadcasted_iota(I32, (devices, 128), 1)
    for part in range(columns // 128):
        staged_ref[...] = updates_ref[:, part * 128 : part * 128 + 128]
        for half in range(rows // 8):
            pieces = [
                staged_ref[pl.ds(half * 8 + k, devices, stride=rows), :]
                for k in range(8)
            ]
            for step in (4, 2, 1):
                upper = ((lane // 16) & step) != 0
                for k in range(8):
                    if k & step:
                        continue
                    a, b = pieces[k], pieces[k + step]
                    pieces[k] = jnp.where(upper, pltpu.roll(b, 16 * step, 1), a)
                    pieces[k + step] = jnp.where(upper, b, pltpu.roll(a, 128 - 16 * step, 1))
            for c in range(8):
                grouped_ref[part * 8 + c, :, half * 128 : half * 128 + 128] = pieces[c].astype(
                    jnp.bfloat16
                )


def project_kernel(
    rows, columns, scale, info_ref, updates_ref, out_ref, grouped_ref, staged_ref, partial_ref
):
    tile = pl.program_id(0)

    @pl.when(tile == 0)
    def _():
        if columns:
            regroup(updates_ref, grouped_ref, staged_ref, rows, columns)
        else:
            grouped_ref[...] = updates_ref[...].astype(jnp.bfloat16)

    lanes = lane_terms(info_ref, tile)
    heights = row_heights(info_ref, rows)
    heights = [jnp.full((16, TILE), h, I32).astype(I16) for h in heights]

    blocks = grouped_ref.shape[0]
    group = math.gcd(blocks, GROUP)

    def add_group(index, total):
        signs, updates = [], []
        for member in range(group):
            block = index * group + member
            height, mixed, carry = column_terms(info_ref, lanes, block)
            for k in range(rows):
                value = (((height + heights[k]) & I16(511)) - I16(256)) ^ mixed
                value = value * short(8 * MUL_B) + carry
                signs.append(jnp.where(value < 0, jnp.bfloat16(-1), jnp.bfloat16(1)))
            updates.append(grouped_ref[block])
        signs = jnp.concatenate(signs, 0)
        updates = jnp.concatenate(updates, 1)
        return total + jnp.dot(updates, signs, preferred_element_type=jnp.float32)

    devices = out_ref.shape[0]
    total = lax.fori_loop(
        0, blocks // group, add_group, jnp.zeros((devices, TILE), jnp.float32)
    )
    here = pl.ds(pl.multiple_of(tile * devices, devices), devices)
    for part in range(TILE // 128):
        partial_ref[part, here, :] = total[:, part * 128 : part * 128 + 128] * scale

    @pl.when(tile == FEAT // TILE - 1)
    def _():
        for device in range(devices):
            for part in range(TILE // 128):
                out_ref[device, :, part * 128 : part * 128 + 128] = partial_ref[
                    part, pl.ds(device, FEAT // TILE, stride=devices), :
                ].astype(jnp.bfloat16)


def project(info, updates, scale):
    m, rows, columns = updates.shape
    blocks = columns // 16
    if rows % 8 == 0 and columns % 128 == 0:
        flat = updates.reshape(m * rows, columns)
        inside = columns
    else:
        flat = updates.reshape(m, rows, blocks, 16).transpose(2, 0, 1, 3)
        flat = flat.reshape(blocks, m, rows * 16)
        inside = 0
    whole = pl.BlockSpec(flat.shape, lambda t, i: (0,) * flat.ndim)
    return pl.pallas_call(
        functools.partial(project_kernel, rows, inside, scale),
        out_shape=jax.ShapeDtypeStruct((m, FEAT // TILE, TILE), jnp.bfloat16),
        grid_spec=pltpu.PrefetchScalarGridSpec(
            num_scalar_prefetch=1,
            grid=(FEAT // TILE,),
            in_specs=[whole],
            out_specs=pl.BlockSpec((m, FEAT // TILE, TILE), lambda t, i: (0, 0, 0)),
            scratch_shapes=[
                pltpu.VMEM((blocks, m, rows * 16), jnp.bfloat16),
                pltpu.VMEM((m * rows, 128), jnp.float32),
                pltpu.VMEM((TILE // 128, FEAT // TILE * m, 128), jnp.float32),
            ],
        ),
        name="project",
    )(info, flat)


def body(
    groups,
    holders,
    acts,
    cotangent,
    down_matrix,
    up_matrix,
    adam_first_moment,
    adam_second_moment,
    lengths,
    sign_hash_salt,
):
    rank, inputs = down_matrix.shape
    rank_rows = 2 * rank
    rows, columns = rank_rows // holders, inputs // groups
    params = rank_rows * inputs
    bound = acts.shape[1] * inputs * 6 * 0.125 * 0.5
    scale = 2.0 ** -max(0, math.ceil(math.log2(bound / 60000)))
    group, holder = lax.axis_index("wide"), lax.axis_index("narrow")

    grads = sequence_grads(groups, holders, acts, cotangent, down_matrix, up_matrix, lengths)
    sent = (grads * scale).astype(jnp.float16)
    grads = lax.all_to_all(sent, AXES, 0, 0, tiled=True).astype(jnp.float32) * (1 / scale)

    def share(moment):
        return lax.dynamic_slice_in_dim(moment.reshape(rows, inputs), group * columns, columns, 1)

    first, second = share(adam_first_moment), share(adam_second_moment)
    moment_one = 0.9 * first[None] + 0.1 * grads
    moment_two = 0.999 * second[None] + 0.001 * grads * grads
    updates = moment_one / (jnp.sqrt(moment_two) + 1e-08)

    info = jnp.stack([sign_hash_salt[0], holder * rows, group * columns])
    partial = project(info, updates, params**-0.5)
    parts = lax.all_to_all(partial, AXES, 0, 0, tiled=True)
    return jnp.sum(parts.astype(jnp.float32), axis=0).reshape(1, FEAT)


def solution(mesh):
    groups, holders = mesh.shape["wide"], mesh.shape["narrow"]
    placed = (
        P(AXES, None, None),
        P(AXES, None, None),
        P(),
        P(),
        P("narrow"),
        P("narrow"),
        P(AXES),
        P(),
    )
    return jax.shard_map(
        functools.partial(body, groups, holders),
        mesh=mesh,
        in_specs=placed,
        out_specs=P(AXES, None),
        check_vma=False,
    )
```

```python
import functools
import math

import jax
import jax.numpy as jnp
import numpy as np
from jax import lax
from jax.experimental import pallas as pl
from jax.experimental.pallas import tpu as pltpu
from jax.sharding import PartitionSpec as P

FEAT = 4096
MUL_A = 747796405
MUL_B = 277803737
AXES = ("wide", "narrow")
COLUMN_BITS = 11
LOW = (1 << COLUMN_BITS) - 1
TILE = 512
EARLY = 5
I16 = jnp.int16
I32 = jnp.int32
SIGN = jnp.float8_e4m3fn


def short(value):
    value &= 0xFFFF
    return np.int16(value - 65536 if value >= 32768 else value)


def grads_kernel(holders, length_ref, acts_ref, cot_ref, down_ref, up_ref, grads_ref):
    groups, (rows, columns) = grads_ref.shape[0] // holders, grads_ref.shape[1:]
    acts = acts_ref[...]
    slots = lax.broadcasted_iota(I32, cot_ref.shape, 0)
    masked = jnp.where(slots < length_ref[0], cot_ref[...].astype(jnp.float32), 0.0)
    masked = masked.astype(jnp.bfloat16)
    last = (((1,), (1,)), ((), ()))
    first = (((0,), (0,)), ((), ()))
    hidden = lax.dot_general(acts, down_ref[...], last, preferred_element_type=jnp.float32)
    inner = lax.dot_general(masked, up_ref[...], last, preferred_element_type=jnp.float32)
    for half, (left, right) in enumerate(((inner, acts), (hidden, masked))):
        grads = lax.dot_general(
            left.astype(jnp.bfloat16), right, first, preferred_element_type=jnp.float32
        )
        for holder in range(holders // 2):
            for group in range(groups):
                grads_ref[group * holders + half * (holders // 2) + holder] = grads[
                    holder * rows : (holder + 1) * rows, group * columns : (group + 1) * columns
                ]


def sequence_grads(groups, holders, acts, cotangent, down_matrix, up_matrix, lengths):
    rank, inputs = down_matrix.shape
    vmem = pl.BlockSpec(memory_space=pltpu.VMEM)
    slabs = (groups * holders, 2 * rank // holders, inputs // groups)
    return pl.pallas_call(
        functools.partial(grads_kernel, holders),
        out_shape=jax.ShapeDtypeStruct(slabs, jnp.float32),
        in_specs=[pl.BlockSpec(memory_space=pltpu.SMEM)] + [vmem] * 4,
        out_specs=vmem,
        name="grads",
    )(lengths, acts[0], cotangent[0], down_matrix, up_matrix.T)


def position():
    return lax.axis_index("wide"), lax.axis_index("narrow")


def lane_terms(salt, tile):
    feature = lax.broadcasted_iota(I32, (8, TILE), 1) + tile * TILE
    product = (feature ^ (salt & (FEAT - 1))) * MUL_A + 1
    low = product & (FEAT - 1)
    high = lax.shift_right_logical(product, 12)

    def packed(x):
        return jnp.concatenate([x, x], 0).astype(I16)

    return (
        packed(high & LOW),
        packed(((high >> COLUMN_BITS) & 511) + 256),
        packed(low >> 8),
        packed((low & 255) << 3),
    )


def column_terms(salt, first, lanes):
    lane_low, lane_high, lane_top, lane_byte = lanes
    column = lax.broadcasted_iota(I32, (16, 128), 0) + first
    product = ((column ^ ((salt >> 12) & LOW)) * MUL_A) & 0xFFFFF
    row_low = (product & LOW).astype(I16)
    row_high = (product >> COLUMN_BITS).astype(I16)
    wide = (1, TILE // 128)
    row_low, row_high = jnp.tile(row_low, wide), jnp.tile(row_high, wide)
    total = row_low + lane_low
    height = row_high + lane_high + lax.shift_right_logical(total, I16(COLUMN_BITS))
    mixed = total * I16(16) + lane_top
    byte8 = (total ^ lane_byte) & I16(0x7F8)
    byte = lax.shift_right_logical(byte8, I16(3))
    tail = byte * I16(MUL_B & 255)
    carry = byte8 * short(MUL_B >> 8) + lax.shift_right_logical(tail, I16(5))
    carry = carry + ((tail * I16(256)) & I16(-32768))
    return height, mixed, carry


def row_heights(salt, rows):
    first = position()[1] * rows
    heights = [(((first + k) ^ (salt >> (12 + COLUMN_BITS))) * MUL_A) & 511 for k in range(rows)]
    return [jnp.full((16, TILE), h, I32).astype(I16) for h in heights]


def block_signs(salt, columns, lanes, heights, block):
    height, mixed, carry = column_terms(salt, position()[0] * columns + block * 16, lanes)
    values = []
    for row in heights:
        value = (((height + row) & I16(511)) - I16(256)) ^ mixed
        values.append(value * short(8 * MUL_B) + carry)
    return jnp.where(jnp.concatenate(values, 0) < 0, SIGN(-1), SIGN(1))


def signs_kernel(rows, columns, first_tile, salt_ref, after_ref, out_ref):
    del after_ref
    salt = salt_ref[0]
    lanes = lane_terms(salt, pl.program_id(0) + first_tile)
    heights = row_heights(salt, rows)
    depth = 16 * rows

    def store(block, _):
        here = pl.ds(pl.multiple_of(block * depth, depth), depth)
        out_ref[0, here, :] = block_signs(salt, columns, lanes, heights, block)
        return 0

    lax.fori_loop(0, columns // 16, store, 0, unroll=2)


def early_signs(salt, rows, columns, after):
    return pl.pallas_call(
        functools.partial(signs_kernel, rows, columns, FEAT // TILE - EARLY),
        out_shape=jax.ShapeDtypeStruct((EARLY, rows * columns, TILE), SIGN),
        grid_spec=pltpu.PrefetchScalarGridSpec(
            num_scalar_prefetch=1,
            grid=(EARLY,),
            in_specs=[pl.BlockSpec(memory_space=pl.ANY)],
            out_specs=pl.BlockSpec((1, rows * columns, TILE), lambda t, i: (t, 0, 0)),
        ),
        cost_estimate=pl.CostEstimate(
            flops=EARLY * rows * columns * TILE * 256, bytes_accessed=0, transcendentals=0
        ),
        name="early_signs",
    )(salt, after)


def regroup(updates_ref, grouped_ref, staged_ref, rows, columns):
    devices = grouped_ref.shape[0]
    lane = lax.broadcasted_iota(I32, (devices, 128), 1)
    for part in range(columns // 128):
        staged_ref[...] = updates_ref[:, part * 128 : part * 128 + 128]
        for half in range(rows // 8):
            pieces = [
                staged_ref[pl.ds(half * 8 + k, devices, stride=rows), :]
                for k in range(8)
            ]
            for step in (4, 2, 1):
                upper = ((lane // 16) & step) != 0
                for k in range(8):
                    if k & step:
                        continue
                    a, b = pieces[k], pieces[k + step]
                    pieces[k] = jnp.where(upper, pltpu.roll(b, 16 * step, 1), a)
                    pieces[k + step] = jnp.where(upper, b, pltpu.roll(a, 128 - 16 * step, 1))
            for c in range(8):
                start = ((part * 8 + c) * rows + half * 8) * 16
                grouped_ref[:, start : start + 128] = pieces[c].astype(jnp.bfloat16)


def project_kernel(
    rows,
    columns,
    scale,
    salt_ref,
    updates_ref,
    early_ref,
    out_ref,
    grouped_ref,
    staged_ref,
    partial_ref,
    signs_ref,
    sems,
):
    tile = pl.program_id(0)
    tiles = FEAT // TILE
    devices = out_ref.shape[0]
    depth = 16 * rows

    def fetch(index):
        return pltpu.make_async_copy(early_ref.at[index], signs_ref.at[index], sems.at[index])

    @pl.when(tile == 0)
    def _():
        for index in range(EARLY):
            fetch(index).start()
        if staged_ref.shape[0] > 8:
            regroup(updates_ref, grouped_ref, staged_ref, rows, columns)
        else:
            grouped_ref[...] = updates_ref[...].astype(jnp.bfloat16)

    def finish(total):
        here = pl.ds(pl.multiple_of(tile * devices, devices), devices)
        for part in range(TILE // 128):
            partial_ref[part, here, :] = total[:, part * 128 : part * 128 + 128] * scale

    @pl.when(tile < tiles - EARLY)
    def _():
        salt = salt_ref[0]
        lanes = lane_terms(salt, tile)
        heights = row_heights(salt, rows)
        signs = [
            block_signs(salt, columns, lanes, heights, block) for block in range(columns // 16)
        ]
        signs = jnp.concatenate(signs, 0)
        finish(jnp.dot(grouped_ref[...], signs, preferred_element_type=jnp.float32))

    @pl.when(tile >= tiles - EARLY)
    def _():
        index = tile - (tiles - EARLY)
        fetch(index).wait()
        finish(jnp.dot(grouped_ref[...], signs_ref[index], preferred_element_type=jnp.float32))

    @pl.when(tile == tiles - 1)
    def _():
        for device in range(devices):
            for part in range(TILE // 128):
                out_ref[device, :, part * 128 : part * 128 + 128] = partial_ref[
                    part, pl.ds(device, tiles, stride=devices), :
                ].astype(jnp.bfloat16)


def project(salt, updates, early, scale):
    m, rows, columns = updates.shape
    if rows % 8 == 0 and columns % 128 == 0:
        flat = updates.reshape(m * rows, columns)
        staged = m * rows
    else:
        flat = updates.reshape(m, rows, columns // 16, 16).transpose(0, 2, 1, 3)
        flat = flat.reshape(m, rows * columns)
        staged = 8
    return pl.pallas_call(
        functools.partial(project_kernel, rows, columns, scale),
        out_shape=jax.ShapeDtypeStruct((m, FEAT // TILE, TILE), jnp.bfloat16),
        grid_spec=pltpu.PrefetchScalarGridSpec(
            num_scalar_prefetch=1,
            grid=(FEAT // TILE,),
            in_specs=[
                pl.BlockSpec(flat.shape, lambda t, i: (0, 0)),
                pl.BlockSpec(memory_space=pl.ANY),
            ],
            out_specs=pl.BlockSpec((m, FEAT // TILE, TILE), lambda t, i: (0, 0, 0)),
            scratch_shapes=[
                pltpu.VMEM((m, rows * columns), jnp.bfloat16),
                pltpu.VMEM((staged, 128), jnp.float32),
                pltpu.VMEM((TILE // 128, FEAT // TILE * m, 128), jnp.float32),
                pltpu.VMEM((EARLY, rows * columns, TILE), SIGN),
                pltpu.SemaphoreType.DMA((EARLY,)),
            ],
        ),
        name="project",
    )(salt, flat, early)


def body(
    groups,
    holders,
    acts,
    cotangent,
    down_matrix,
    up_matrix,
    adam_first_moment,
    adam_second_moment,
    lengths,
    sign_hash_salt,
):
    rank, inputs = down_matrix.shape
    rank_rows = 2 * rank
    rows, columns = rank_rows // holders, inputs // groups
    params = rank_rows * inputs
    bound = acts.shape[1] * inputs * 6 * 0.125 * 0.5
    scale = 2.0 ** -max(0, math.ceil(math.log2(bound / 60000)))
    group = lax.axis_index("wide")

    slabs = sequence_grads(groups, holders, acts, cotangent, down_matrix, up_matrix, lengths)
    sent = (slabs * scale).astype(jnp.float16)
    early = early_signs(sign_hash_salt, rows, columns, slabs)
    grads = lax.all_to_all(sent, AXES, 0, 0, tiled=True).astype(jnp.float32) * (1 / scale)

    def share(moment):
        return lax.dynamic_slice_in_dim(moment.reshape(rows, inputs), group * columns, columns, 1)

    first, second = share(adam_first_moment), share(adam_second_moment)
    moment_one = 0.9 * first[None] + 0.1 * grads
    moment_two = 0.999 * second[None] + 0.001 * grads * grads
    updates = moment_one / (jnp.sqrt(moment_two) + 1e-08)

    partial = project(sign_hash_salt, updates, early, params**-0.5)
    parts = lax.all_to_all(partial, AXES, 0, 0, tiled=True)
    return jnp.sum(parts.astype(jnp.float32), axis=0).reshape(1, FEAT)


def solution(mesh):
    groups, holders = mesh.shape["wide"], mesh.shape["narrow"]
    placed = (
        P(AXES, None, None),
        P(AXES, None, None),
        P(),
        P(),
        P("narrow"),
        P("narrow"),
        P(AXES),
        P(),
    )
    return jax.shard_map(
        functools.partial(body, groups, holders),
        mesh=mesh,
        in_specs=placed,
        out_specs=P(AXES, None),
        check_vma=False,
    )
```

```python
import functools
import math

import jax
import jax.numpy as jnp
import numpy as np
from jax import lax
from jax.experimental import pallas as pl
from jax.experimental.pallas import tpu as pltpu
from jax.sharding import PartitionSpec as P

FEAT = 4096
MUL_A = 747796405
MUL_B = 277803737
AXES = ("wide", "narrow")
COLUMN_BITS = 11
LOW = (1 << COLUMN_BITS) - 1
TILE = 512
GROUP = 2
EARLY = 5
I16 = jnp.int16
I32 = jnp.int32
SIGN = jnp.float8_e4m3fn


def short(value):
    value &= 0xFFFF
    return np.int16(value - 65536 if value >= 32768 else value)


def grads_kernel(holders, length_ref, acts_ref, cot_ref, down_ref, up_ref, grads_ref):
    groups, (rows, columns) = grads_ref.shape[0] // holders, grads_ref.shape[1:]
    acts = acts_ref[...]
    slots = lax.broadcasted_iota(I32, cot_ref.shape, 0)
    masked = jnp.where(slots < length_ref[0], cot_ref[...].astype(jnp.float32), 0.0)
    masked = masked.astype(jnp.bfloat16)
    last = (((1,), (1,)), ((), ()))
    first = (((0,), (0,)), ((), ()))
    hidden = lax.dot_general(acts, down_ref[...], last, preferred_element_type=jnp.float32)
    inner = lax.dot_general(masked, up_ref[...], last, preferred_element_type=jnp.float32)
    for half, (left, right) in enumerate(((inner, acts), (hidden, masked))):
        grads = lax.dot_general(
            left.astype(jnp.bfloat16), right, first, preferred_element_type=jnp.float32
        )
        for holder in range(holders // 2):
            for group in range(groups):
                grads_ref[group * holders + half * (holders // 2) + holder] = grads[
                    holder * rows : (holder + 1) * rows, group * columns : (group + 1) * columns
                ]


def sequence_grads(groups, holders, acts, cotangent, down_matrix, up_matrix, lengths):
    rank, inputs = down_matrix.shape
    vmem = pl.BlockSpec(memory_space=pltpu.VMEM)
    slabs = (groups * holders, 2 * rank // holders, inputs // groups)
    return pl.pallas_call(
        functools.partial(grads_kernel, holders),
        out_shape=jax.ShapeDtypeStruct(slabs, jnp.float32),
        in_specs=[pl.BlockSpec(memory_space=pltpu.SMEM)] + [vmem] * 4,
        out_specs=vmem,
        name="grads",
    )(lengths, acts[0], cotangent[0], down_matrix, up_matrix.T)


def position():
    return lax.axis_index("wide"), lax.axis_index("narrow")


def lane_terms(salt, tile):
    feature = lax.broadcasted_iota(I32, (8, TILE), 1) + tile * TILE
    product = (feature ^ (salt & (FEAT - 1))) * MUL_A + 1
    low = product & (FEAT - 1)
    high = lax.shift_right_logical(product, 12)

    def packed(x):
        return jnp.concatenate([x, x], 0).astype(I16)

    return (
        packed(high & LOW),
        packed(((high >> COLUMN_BITS) & 511) + 256),
        packed(low >> 8),
        packed((low & 255) << 3),
    )


def column_terms(salt, first, lanes):
    lane_low, lane_high, lane_top, lane_byte = lanes
    column = lax.broadcasted_iota(I32, (16, 128), 0) + first
    product = ((column ^ ((salt >> 12) & LOW)) * MUL_A) & 0xFFFFF
    row_low = (product & LOW).astype(I16)
    row_high = (product >> COLUMN_BITS).astype(I16)
    wide = (1, TILE // 128)
    row_low, row_high = jnp.tile(row_low, wide), jnp.tile(row_high, wide)
    total = row_low + lane_low
    height = row_high + lane_high + lax.shift_right_logical(total, I16(COLUMN_BITS))
    mixed = total * I16(16) + lane_top
    byte8 = (total ^ lane_byte) & I16(0x7F8)
    byte = lax.shift_right_logical(byte8, I16(3))
    tail = byte * I16(MUL_B & 255)
    carry = byte8 * short(MUL_B >> 8) + lax.shift_right_logical(tail, I16(5))
    carry = carry + ((tail * I16(256)) & I16(-32768))
    return height, mixed, carry


def row_heights(salt, rows):
    first = position()[1] * rows
    heights = [(((first + k) ^ (salt >> (12 + COLUMN_BITS))) * MUL_A) & 511 for k in range(rows)]
    return [jnp.full((16, TILE), h, I32).astype(I16) for h in heights]


def block_signs(salt, columns, lanes, heights, block):
    height, mixed, carry = column_terms(salt, position()[0] * columns + block * 16, lanes)
    values = []
    for row in heights:
        value = (((height + row) & I16(511)) - I16(256)) ^ mixed
        values.append(value * short(8 * MUL_B) + carry)
    return jnp.where(jnp.concatenate(values, 0) < 0, SIGN(-1), SIGN(1))


def signs_kernel(
    rows, columns, first_tile, salt_ref, after_ref, first_ref, second_ref, out_ref, one_ref, two_ref
):
    del after_ref
    salt = salt_ref[0]
    lanes = lane_terms(salt, pl.program_id(0) + first_tile)
    heights = row_heights(salt, rows)
    depth = 16 * rows

    @pl.when(pl.program_id(0) == 0)
    def _():
        stride = first_ref.shape[0] // rows
        for part in range(columns // 128):
            here = pl.ds(position()[0] * (columns // 128) + part, rows, stride=stride)
            one_ref[:, part * 128 : part * 128 + 128] = first_ref[here, :]
            two_ref[:, part * 128 : part * 128 + 128] = second_ref[here, :]

    def store(block, _):
        here = pl.ds(pl.multiple_of(block * depth, depth), depth)
        out_ref[0, here, :] = block_signs(salt, columns, lanes, heights, block)
        return 0

    lax.fori_loop(0, columns // 16, store, 0, unroll=2)


def early_signs(salt, rows, columns, after, first, second):
    whole = pl.BlockSpec((first.size // 128, 128), lambda t, i: (0, 0))
    share = pl.BlockSpec((rows, columns), lambda t, i: (0, 0))
    moment = jax.ShapeDtypeStruct((rows, columns), jnp.float32)
    return pl.pallas_call(
        functools.partial(signs_kernel, rows, columns, FEAT // TILE - EARLY),
        out_shape=(
            jax.ShapeDtypeStruct((EARLY, rows * columns, TILE), SIGN),
            moment,
            moment,
        ),
        grid_spec=pltpu.PrefetchScalarGridSpec(
            num_scalar_prefetch=1,
            grid=(EARLY,),
            in_specs=[pl.BlockSpec(memory_space=pl.ANY), whole, whole],
            out_specs=(
                pl.BlockSpec((1, rows * columns, TILE), lambda t, i: (t, 0, 0)),
                share,
                share,
            ),
        ),
        cost_estimate=pl.CostEstimate(
            flops=EARLY * rows * columns * TILE * 256, bytes_accessed=0, transcendentals=0
        ),
        name="early_signs",
    )(salt, after, first.reshape(-1, 128), second.reshape(-1, 128))


def regroup(updates_ref, grouped_ref, staged_ref, rows, columns):
    devices = grouped_ref.shape[0]
    lane = lax.broadcasted_iota(I32, (devices, 128), 1)
    for part in range(columns // 128):
        staged_ref[...] = updates_ref[:, part * 128 : part * 128 + 128]
        for half in range(rows // 8):
            pieces = [
                staged_ref[pl.ds(half * 8 + k, devices, stride=rows), :]
                for k in range(8)
            ]
            for step in (4, 2, 1):
                upper = ((lane // 16) & step) != 0
                for k in range(8):
                    if k & step:
                        continue
                    a, b = pieces[k], pieces[k + step]
                    pieces[k] = jnp.where(upper, pltpu.roll(b, 16 * step, 1), a)
                    pieces[k + step] = jnp.where(upper, b, pltpu.roll(a, 128 - 16 * step, 1))
            for c in range(8):
                start = ((part * 8 + c) * rows + half * 8) * 16
                grouped_ref[:, start : start + 128] = pieces[c].astype(jnp.bfloat16)


def project_kernel(
    rows,
    columns,
    scale,
    salt_ref,
    updates_ref,
    early_ref,
    out_ref,
    grouped_ref,
    staged_ref,
    partial_ref,
    signs_ref,
    sems,
):
    devices = out_ref.shape[0]
    late = FEAT // TILE - EARLY

    def fetch(index):
        return pltpu.make_async_copy(early_ref.at[index], signs_ref.at[index], sems.at[index])

    def product(start, signs):
        updates = grouped_ref[:, start : start + signs.shape[0]]
        return jnp.dot(updates, signs, preferred_element_type=jnp.float32)

    def finish(tile, total):
        total = total * scale
        for part in range(TILE // 128):
            start = (tile * (TILE // 128) + part) * devices
            partial_ref[start : start + devices, :] = total[:, part * 128 : part * 128 + 128]

    for index in range(EARLY):
        fetch(index).start()
    if staged_ref.shape[0] > 8:
        regroup(updates_ref, grouped_ref, staged_ref, rows, columns)
    else:
        grouped_ref[...] = updates_ref[...].astype(jnp.bfloat16)

    salt = salt_ref[0]
    heights = row_heights(salt, rows)
    done = 0
    for tile in range(late):
        ready = EARLY * tile // max(late - 1, 1)
        for index in range(done, ready):
            fetch(index).wait()
        lanes = lane_terms(salt, tile)
        totals = [0.0] * (1 + ready - done)
        blocks = columns // 16
        group = math.gcd(blocks, GROUP)
        for block in range(0, blocks, group):
            start, size = block * rows * 16, group * rows * 16
            for index in range(done, ready):
                stored = signs_ref[index, start : start + size, :]
                totals[1 + index - done] += product(start, stored)
            signs = [
                block_signs(salt, columns, lanes, heights, block + member)
                for member in range(group)
            ]
            totals[0] += product(start, jnp.concatenate(signs, 0))
        finish(tile, totals[0])
        for index in range(done, ready):
            finish(late + index, totals[1 + index - done])
        done = ready

    for device in range(devices):
        out_ref[device] = partial_ref[
            pl.ds(device, FEAT // 128, stride=devices), :
        ].astype(jnp.bfloat16)


def project(salt, updates, early, scale):
    m, rows, columns = updates.shape
    if rows % 8 == 0 and columns % 128 == 0:
        flat = updates.reshape(m * rows, columns)
        staged = m * rows
    else:
        flat = updates.reshape(m, rows, columns // 16, 16).transpose(0, 2, 1, 3)
        flat = flat.reshape(m, rows * columns)
        staged = 8
    return pl.pallas_call(
        functools.partial(project_kernel, rows, columns, scale),
        out_shape=jax.ShapeDtypeStruct((m, FEAT // 128, 128), jnp.bfloat16),
        in_specs=[
            pl.BlockSpec(memory_space=pltpu.SMEM),
            pl.BlockSpec(memory_space=pltpu.VMEM),
            pl.BlockSpec(memory_space=pl.ANY),
        ],
        out_specs=pl.BlockSpec(memory_space=pltpu.VMEM),
        scratch_shapes=[
            pltpu.VMEM((m, rows * columns), jnp.bfloat16),
            pltpu.VMEM((staged, 128), jnp.float32),
            pltpu.VMEM((FEAT // 128 * m, 128), jnp.float32),
            pltpu.VMEM((EARLY, rows * columns, TILE), SIGN),
            pltpu.SemaphoreType.DMA((EARLY,)),
        ],
        name="project",
    )(salt, flat, early)


def body(
    groups,
    holders,
    acts,
    cotangent,
    down_matrix,
    up_matrix,
    adam_first_moment,
    adam_second_moment,
    lengths,
    sign_hash_salt,
):
    rank, inputs = down_matrix.shape
    rank_rows = 2 * rank
    rows, columns = rank_rows // holders, inputs // groups
    params = rank_rows * inputs
    bound = acts.shape[1] * inputs * 6 * 0.125 * 0.5
    scale = 2.0 ** -max(0, math.ceil(math.log2(bound / 60000)))

    slabs = sequence_grads(groups, holders, acts, cotangent, down_matrix, up_matrix, lengths)
    sent = (slabs * scale).astype(jnp.float16)
    early, first, second = early_signs(
        sign_hash_salt, rows, columns, slabs, adam_first_moment, adam_second_moment
    )
    grads = lax.all_to_all(sent, AXES, 0, 0, tiled=True).astype(jnp.float32) * (1 / scale)

    moment_one = 0.9 * first[None] + 0.1 * grads
    moment_two = 0.999 * second[None] + 0.001 * grads * grads
    updates = moment_one / (jnp.sqrt(moment_two) + 1e-08)

    partial = project(sign_hash_salt, updates, early, params**-0.5)
    parts = lax.all_to_all(partial, AXES, 0, 0, tiled=True)
    return jnp.sum(parts.astype(jnp.float32), axis=0).reshape(1, FEAT)


def solution(mesh):
    groups, holders = mesh.shape["wide"], mesh.shape["narrow"]
    placed = (
        P(AXES, None, None),
        P(AXES, None, None),
        P(),
        P(),
        P("narrow"),
        P("narrow"),
        P(AXES),
        P(),
    )
    return jax.shard_map(
        functools.partial(body, groups, holders),
        mesh=mesh,
        in_specs=placed,
        out_specs=P(AXES, None),
        check_vma=False,
    )
```

```python
import functools
import math

import jax
import jax.numpy as jnp
import numpy as np
from jax import lax
from jax.experimental import pallas as pl
from jax.experimental.pallas import tpu as pltpu
from jax.sharding import PartitionSpec as P

FEAT = 4096
MUL_A = 747796405
MUL_B = 277803737
AXES = ("wide", "narrow")
COLUMN_BITS = 11
LOW = (1 << COLUMN_BITS) - 1
TILE = 512
GROUP = 2
AHEAD = 2
EARLY = 5
I16 = jnp.int16
I32 = jnp.int32
SIGN = jnp.float8_e4m3fn


def short(value):
    value &= 0xFFFF
    return np.int16(value - 65536 if value >= 32768 else value)


def grads_kernel(holders, length_ref, acts_ref, cot_ref, down_ref, up_ref, grads_ref):
    groups, (rows, columns) = grads_ref.shape[0] // holders, grads_ref.shape[1:]
    acts = acts_ref[...]
    slots = lax.broadcasted_iota(I32, cot_ref.shape, 0)
    masked = jnp.where(slots < length_ref[0], cot_ref[...].astype(jnp.float32), 0.0)
    masked = masked.astype(jnp.bfloat16)
    last = (((1,), (1,)), ((), ()))
    first = (((0,), (0,)), ((), ()))
    hidden = lax.dot_general(acts, down_ref[...], last, preferred_element_type=jnp.float32)
    inner = lax.dot_general(masked, up_ref[...], last, preferred_element_type=jnp.float32)
    for half, (left, right) in enumerate(((inner, acts), (hidden, masked))):
        grads = lax.dot_general(
            left.astype(jnp.bfloat16), right, first, preferred_element_type=jnp.float32
        )
        for holder in range(holders // 2):
            for group in range(groups):
                grads_ref[group * holders + half * (holders // 2) + holder] = grads[
                    holder * rows : (holder + 1) * rows, group * columns : (group + 1) * columns
                ].astype(jnp.bfloat16)


def sequence_grads(groups, holders, acts, cotangent, down_matrix, up_matrix, lengths):
    rank, inputs = down_matrix.shape
    vmem = pl.BlockSpec(memory_space=pltpu.VMEM)
    slabs = (groups * holders, 2 * rank // holders, inputs // groups)
    return pl.pallas_call(
        functools.partial(grads_kernel, holders),
        out_shape=jax.ShapeDtypeStruct(slabs, jnp.bfloat16),
        in_specs=[pl.BlockSpec(memory_space=pltpu.SMEM)] + [vmem] * 4,
        out_specs=vmem,
        name="grads",
    )(lengths, acts[0], cotangent[0], down_matrix, up_matrix.T)


def position():
    return lax.axis_index("wide"), lax.axis_index("narrow")


def lane_terms(salt, tile):
    feature = lax.broadcasted_iota(I32, (8, TILE), 1) + tile * TILE
    product = (feature ^ (salt & (FEAT - 1))) * MUL_A + 1
    low = product & (FEAT - 1)
    high = lax.shift_right_logical(product, 12)

    def packed(x):
        return jnp.concatenate([x, x], 0).astype(I16)

    return (
        packed(high & LOW),
        packed(((high >> COLUMN_BITS) & 511) + 256),
        packed(low >> 8),
        packed((low & 255) << 3),
    )


def column_terms(salt, first, lanes):
    lane_low, lane_high, lane_top, lane_byte = lanes
    column = lax.broadcasted_iota(I32, (16, 128), 0) + first
    product = ((column ^ ((salt >> 12) & LOW)) * MUL_A) & 0xFFFFF
    row_low = (product & LOW).astype(I16)
    row_high = (product >> COLUMN_BITS).astype(I16)
    wide = (1, TILE // 128)
    row_low, row_high = jnp.tile(row_low, wide), jnp.tile(row_high, wide)
    total = row_low + lane_low
    height = row_high + lane_high + lax.shift_right_logical(total, I16(COLUMN_BITS))
    mixed = total * I16(16) + lane_top
    byte8 = (total ^ lane_byte) & I16(0x7F8)
    byte = lax.shift_right_logical(byte8, I16(3))
    tail = byte * I16(MUL_B & 255)
    carry = byte8 * short(MUL_B >> 8) + lax.shift_right_logical(tail, I16(5))
    carry = carry + ((tail * I16(256)) & I16(-32768))
    return height, mixed, carry


def row_heights(salt, rows):
    first = position()[1] * rows
    heights = [(((first + k) ^ (salt >> (12 + COLUMN_BITS))) * MUL_A) & 511 for k in range(rows)]
    return [jnp.full((16, TILE), h, I32).astype(I16) for h in heights]


def block_signs(salt, columns, lanes, heights, block):
    height, mixed, carry = column_terms(salt, position()[0] * columns + block * 16, lanes)
    values = []
    for row in heights:
        value = (((height + row) & I16(511)) - I16(256)) ^ mixed
        values.append(value * short(8 * MUL_B) + carry)
    return jnp.where(jnp.concatenate(values, 0) < 0, SIGN(-1), SIGN(1))


def signs_kernel(rows, columns, salt_ref, after_ref, out_ref):
    del after_ref
    salt = salt_ref[0]
    lanes = lane_terms(salt, pl.program_id(0) + FEAT // TILE - EARLY)
    heights = row_heights(salt, rows)
    depth = 16 * rows
    blocks = out_ref.shape[1] // depth
    first = pl.program_id(1) * blocks

    def store(block, _):
        here = pl.ds(pl.multiple_of(block * depth, depth), depth)
        out_ref[0, here, :] = block_signs(salt, columns, lanes, heights, first + block)
        return 0

    lax.fori_loop(0, blocks, store, 0, unroll=2)


def early_signs(salt, rows, columns, after):
    size = rows * columns
    return pl.pallas_call(
        functools.partial(signs_kernel, rows, columns),
        out_shape=jax.ShapeDtypeStruct((EARLY, size, TILE), SIGN),
        grid_spec=pltpu.PrefetchScalarGridSpec(
            num_scalar_prefetch=1,
            grid=(EARLY, 2),
            in_specs=[pl.BlockSpec(memory_space=pl.ANY)],
            out_specs=pl.BlockSpec((1, size // 2, TILE), lambda t, h, i: (t, h, 0)),
        ),
        cost_estimate=pl.CostEstimate(
            flops=EARLY * size * TILE * 256, bytes_accessed=0, transcendentals=0
        ),
        name="early_signs",
    )(salt, after)


def adam_scale(grads, first, second):
    moment_one = 0.9 * first + 0.1 * grads
    moment_two = 0.999 * second + 0.001 * grads * grads
    return moment_one / (jnp.sqrt(moment_two) + 1e-08)


def keep(updates, grouped_ref, start):
    devices, size = updates.shape
    high = updates.astype(jnp.bfloat16)
    grouped_ref[:devices, start : start + size] = high
    low = updates - high.astype(jnp.float32)
    grouped_ref[devices:, start : start + size] = low.astype(jnp.bfloat16)


def regroup(rows, grads_ref, first_ref, second_ref, grouped_ref, staged_ref):
    columns = grads_ref.shape[1]
    devices = grads_ref.shape[0] // rows
    stride = first_ref.shape[0] // rows
    lane = lax.broadcasted_iota(I32, (devices, 128), 1)
    for part in range(columns // 128):
        lanes = slice(part * 128, part * 128 + 128)
        share = pl.ds(position()[0] * (columns // 128) + part, rows, stride=stride)
        first, second = first_ref[share, :], second_ref[share, :]
        for device in range(devices):
            here = slice(device * rows, (device + 1) * rows)
            grads = grads_ref[here, lanes].astype(jnp.float32)
            staged_ref[here, :] = adam_scale(grads, first, second)
        for half in range(rows // 8):
            pieces = [
                staged_ref[pl.ds(half * 8 + k, devices, stride=rows), :] for k in range(8)
            ]
            for step in (4, 2, 1):
                upper = ((lane // 16) & step) != 0
                for k in range(8):
                    if k & step:
                        continue
                    a, b = pieces[k], pieces[k + step]
                    pieces[k] = jnp.where(upper, pltpu.roll(b, 16 * step, 1), a)
                    pieces[k + step] = jnp.where(upper, b, pltpu.roll(a, 128 - 16 * step, 1))
            for c in range(8):
                keep(pieces[c], grouped_ref, ((part * 8 + c) * rows + half * 8) * 16)


def project_kernel(
    rows,
    columns,
    scale,
    salt_ref,
    early_ref,
    grads_ref,
    *refs,
):
    out_ref, grouped_ref, staged_ref, partial_ref, signs_ref, sems = refs[-6:]
    devices = out_ref.shape[0]
    late = FEAT // TILE - EARLY

    def fetch(index):
        return pltpu.make_async_copy(early_ref.at[index], signs_ref.at[index], sems.at[index])

    for index in range(min(EARLY, AHEAD)):
        fetch(index).start()

    def product(start, signs):
        updates = grouped_ref[:, start : start + signs.shape[0]]
        return jnp.dot(updates, signs, preferred_element_type=jnp.float32)

    def finish(tile, total):
        total = (total[:devices] + total[devices:]) * scale
        for part in range(TILE // 128):
            start = (tile * (TILE // 128) + part) * devices
            partial_ref[start : start + devices, :] = total[:, part * 128 : part * 128 + 128]

    if len(refs) > 6:
        regroup(rows, grads_ref, *refs[:2], grouped_ref, staged_ref)
    else:
        keep(grads_ref[...], grouped_ref, 0)

    salt = salt_ref[0]
    heights = row_heights(salt, rows)
    done = 0
    for tile in range(late):
        ready = EARLY if tile == late - 1 else min(EARLY, AHEAD * tile)
        for index in range(max(done, AHEAD), ready):
            fetch(index).wait()
        lanes = lane_terms(salt, tile)
        totals = [0.0] * (1 + ready - done)
        blocks = columns // 16
        group = math.gcd(blocks, GROUP)
        for block in range(0, blocks, group):
            if tile == 0 and block == blocks // 2:
                for index in range(min(EARLY, AHEAD)):
                    fetch(index).wait()
                for index in range(AHEAD, EARLY):
                    fetch(index).start()
            start, size = block * rows * 16, group * rows * 16
            for index in range(done, ready):
                stored = signs_ref[index, start : start + size, :]
                totals[1 + index - done] += product(start, stored)
            signs = [
                block_signs(salt, columns, lanes, heights, block + member)
                for member in range(group)
            ]
            totals[0] += product(start, jnp.concatenate(signs, 0))
        finish(tile, totals[0])
        for index in range(done, ready):
            finish(late + index, totals[1 + index - done])
        done = ready

    for device in range(devices):
        out_ref[device] = partial_ref[
            pl.ds(device, FEAT // 128, stride=devices), :
        ].astype(jnp.bfloat16)


def project(salt, grads, first, second, early, scale):
    m, rows, columns = grads.shape
    vmem = pl.BlockSpec(memory_space=pltpu.VMEM)
    if rows % 16 == 0 and columns % 128 == 0:
        first, second = first.reshape(-1, 128), second.reshape(-1, 128)
        operands = (grads.reshape(m * rows, columns), first, second)
    else:

        def share(moment):
            start = lax.axis_index("wide") * columns
            return lax.dynamic_slice_in_dim(moment.reshape(rows, -1), start, columns, 1)

        flat = adam_scale(grads.astype(jnp.float32), share(first)[None], share(second)[None])
        flat = flat.reshape(m, rows, columns // 16, 16).transpose(0, 2, 1, 3)
        operands = (flat.reshape(m, rows * columns),)
    return pl.pallas_call(
        functools.partial(project_kernel, rows, columns, scale),
        out_shape=jax.ShapeDtypeStruct((m, FEAT // 128, 128), jnp.bfloat16),
        in_specs=[
            pl.BlockSpec(memory_space=pltpu.SMEM),
            pl.BlockSpec(memory_space=pl.ANY),
        ]
        + [vmem] * len(operands),
        out_specs=vmem,
        scratch_shapes=[
            pltpu.VMEM((2 * m, rows * columns), jnp.bfloat16),
            pltpu.VMEM((m * rows, 128), jnp.float32),
            pltpu.VMEM((FEAT // 128 * m, 128), jnp.float32),
            pltpu.VMEM((EARLY, rows * columns, TILE), SIGN),
            pltpu.SemaphoreType.DMA((EARLY,)),
        ],
        compiler_params=pltpu.CompilerParams(vmem_limit_bytes=44 << 20),
        name="project",
    )(salt, early, *operands)


def body(
    groups,
    holders,
    acts,
    cotangent,
    down_matrix,
    up_matrix,
    adam_first_moment,
    adam_second_moment,
    lengths,
    sign_hash_salt,
):
    rank, inputs = down_matrix.shape
    rank_rows = 2 * rank
    rows, columns = rank_rows // holders, inputs // groups
    params = rank_rows * inputs
    slabs = sequence_grads(groups, holders, acts, cotangent, down_matrix, up_matrix, lengths)
    early = early_signs(sign_hash_salt, rows, columns, slabs)
    grads = lax.all_to_all(slabs, AXES, 0, 0, tiled=True)
    partial = project(
        sign_hash_salt, grads, adam_first_moment, adam_second_moment, early, params**-0.5
    )
    parts = lax.all_to_all(partial, AXES, 0, 0, tiled=True)
    return jnp.sum(parts.astype(jnp.float32), axis=0).reshape(1, FEAT)


def solution(mesh):
    groups, holders = mesh.shape["wide"], mesh.shape["narrow"]
    placed = (
        P(AXES, None, None),
        P(AXES, None, None),
        P(),
        P(),
        P("narrow"),
        P("narrow"),
        P(AXES),
        P(),
    )
    return jax.shard_map(
        functools.partial(body, groups, holders),
        mesh=mesh,
        in_specs=placed,
        out_specs=P(AXES, None),
        check_vma=False,
    )
```

```python
import functools
import math

import jax
import jax.numpy as jnp
import numpy as np
from jax import lax
from jax.experimental import pallas as pl
from jax.experimental.pallas import tpu as pltpu
from jax.sharding import PartitionSpec as P

FEAT = 4096
MUL_A = 747796405
MUL_B = 277803737
AXES = ("wide", "narrow")
COLUMN_BITS = 11
LOW = (1 << COLUMN_BITS) - 1
TILE = 512
GROUP = 2
SPLIT = 8
FIRST, EACH = 5, 9
AHEAD = 3
EARLY = 5
I16 = jnp.int16
I32 = jnp.int32
SIGN = jnp.float8_e4m3fn


def short(value):
    value &= 0xFFFF
    return np.int16(value - 65536 if value >= 32768 else value)


def grads_kernel(holders, length_ref, acts_ref, cot_ref, down_ref, up_ref, grads_ref):
    groups, (rows, columns) = grads_ref.shape[0] // holders, grads_ref.shape[1:]
    acts = acts_ref[...]
    slots = lax.broadcasted_iota(I32, cot_ref.shape, 0)
    masked = jnp.where(slots < length_ref[0], cot_ref[...].astype(jnp.float32), 0.0)
    masked = masked.astype(jnp.bfloat16)
    last = (((1,), (1,)), ((), ()))
    first = (((0,), (0,)), ((), ()))
    hidden = lax.dot_general(acts, down_ref[...], last, preferred_element_type=jnp.float32)
    inner = lax.dot_general(masked, up_ref[...], last, preferred_element_type=jnp.float32)
    for half, (left, right) in enumerate(((inner, acts), (hidden, masked))):
        grads = lax.dot_general(
            left.astype(jnp.bfloat16), right, first, preferred_element_type=jnp.float32
        )
        for holder in range(holders // 2):
            for group in range(groups):
                grads_ref[group * holders + half * (holders // 2) + holder] = grads[
                    holder * rows : (holder + 1) * rows, group * columns : (group + 1) * columns
                ].astype(jnp.bfloat16)


def sequence_grads(groups, holders, acts, cotangent, down_matrix, up_matrix, lengths):
    rank, inputs = down_matrix.shape
    vmem = pl.BlockSpec(memory_space=pltpu.VMEM)
    slabs = (groups * holders, 2 * rank // holders, inputs // groups)
    return pl.pallas_call(
        functools.partial(grads_kernel, holders),
        out_shape=jax.ShapeDtypeStruct(slabs, jnp.bfloat16),
        in_specs=[pl.BlockSpec(memory_space=pltpu.SMEM)] + [vmem] * 4,
        out_specs=vmem,
        name="grads",
    )(lengths, acts[0], cotangent[0], down_matrix, up_matrix.T)


def position():
    return lax.axis_index("wide"), lax.axis_index("narrow")


def lane_terms(salt, tile):
    feature = lax.broadcasted_iota(I32, (8, TILE), 1) + tile * TILE
    product = (feature ^ (salt & (FEAT - 1))) * MUL_A + 1
    low = product & (FEAT - 1)
    high = lax.shift_right_logical(product, 12)

    def packed(x):
        return jnp.concatenate([x, x], 0).astype(I16)

    return (
        packed(high & LOW),
        packed(((high >> COLUMN_BITS) & 511) + 256),
        packed(low >> 8),
        packed((low & 255) << 3),
    )


def column_terms(salt, first, lanes):
    lane_low, lane_high, lane_top, lane_byte = lanes
    column = lax.broadcasted_iota(I32, (16, 128), 0) + first
    product = ((column ^ ((salt >> 12) & LOW)) * MUL_A) & 0xFFFFF
    row_low = (product & LOW).astype(I16)
    row_high = (product >> COLUMN_BITS).astype(I16)
    wide = (1, TILE // 128)
    row_low, row_high = jnp.tile(row_low, wide), jnp.tile(row_high, wide)
    total = row_low + lane_low
    height = row_high + lane_high + lax.shift_right_logical(total, I16(COLUMN_BITS))
    mixed = total * I16(16) + lane_top
    byte8 = (total ^ lane_byte) & I16(0x7F8)
    byte = lax.shift_right_logical(byte8, I16(3))
    tail = byte * I16(MUL_B & 255)
    carry = byte8 * short(MUL_B >> 8) + lax.shift_right_logical(tail, I16(5))
    carry = carry + ((tail * I16(256)) & I16(-32768))
    return height, mixed, carry


def row_heights(salt, rows):
    first = position()[1] * rows
    heights = [(((first + k) ^ (salt >> (12 + COLUMN_BITS))) * MUL_A) & 511 for k in range(rows)]
    return [jnp.full((16, TILE), h, I32).astype(I16) for h in heights]


def block_signs(salt, columns, lanes, heights, block):
    height, mixed, carry = column_terms(salt, position()[0] * columns + block * 16, lanes)
    values = []
    for row in heights:
        value = (((height + row) & I16(511)) - I16(256)) ^ mixed
        values.append(value * short(8 * MUL_B) + carry)
    return jnp.where(jnp.concatenate(values, 0) < 0, SIGN(-1), SIGN(1))


def signs_kernel(rows, columns, salt_ref, after_ref, out_ref):
    del after_ref
    salt = salt_ref[0]
    lanes = lane_terms(salt, pl.program_id(0) + FEAT // TILE - EARLY)
    heights = row_heights(salt, rows)
    depth = 16 * rows
    blocks = out_ref.shape[1] // depth
    first = pl.program_id(1) * blocks

    def store(block, _):
        here = pl.ds(pl.multiple_of(block * depth, depth), depth)
        out_ref[0, here, :] = block_signs(salt, columns, lanes, heights, first + block)
        return 0

    lax.fori_loop(0, blocks, store, 0, unroll=2)


def early_signs(salt, rows, columns, after):
    size = rows * columns
    return pl.pallas_call(
        functools.partial(signs_kernel, rows, columns),
        out_shape=jax.ShapeDtypeStruct((EARLY, size, TILE), SIGN),
        grid_spec=pltpu.PrefetchScalarGridSpec(
            num_scalar_prefetch=1,
            grid=(EARLY, 2),
            in_specs=[pl.BlockSpec(memory_space=pl.ANY)],
            out_specs=pl.BlockSpec((1, size // 2, TILE), lambda t, h, i: (t, h, 0)),
        ),
        cost_estimate=pl.CostEstimate(
            flops=EARLY * size * TILE * 256, bytes_accessed=0, transcendentals=0
        ),
        name="early_signs",
    )(salt, after)


def adam_scale(grads, first, second):
    moment_one = 0.9 * first + 0.1 * grads
    moment_two = 0.999 * second + 0.001 * grads * grads
    return moment_one / (jnp.sqrt(moment_two) + 1e-08)


def keep(updates, grouped_ref, start):
    devices, size = updates.shape
    high = updates.astype(jnp.bfloat16)
    grouped_ref[:devices, start : start + size] = high
    low = updates - high.astype(jnp.float32)
    grouped_ref[devices:, start : start + size] = low.astype(jnp.bfloat16)


def regroup(rows, grads_ref, first_ref, second_ref, grouped_ref, staged_ref):
    columns = grads_ref.shape[1]
    devices = grads_ref.shape[0] // rows
    stride = first_ref.shape[0] // rows
    lane = lax.broadcasted_iota(I32, (devices, 128), 1)
    for part in range(columns // 128):
        lanes = slice(part * 128, part * 128 + 128)
        share = pl.ds(position()[0] * (columns // 128) + part, rows, stride=stride)
        first, second = first_ref[share, :], second_ref[share, :]
        for device in range(devices):
            here = slice(device * rows, (device + 1) * rows)
            grads = grads_ref[here, lanes].astype(jnp.float32)
            staged_ref[here, :] = adam_scale(grads, first, second)
        for half in range(rows // 8):
            pieces = [
                staged_ref[pl.ds(half * 8 + k, devices, stride=rows), :] for k in range(8)
            ]
            for step in (4, 2, 1):
                upper = ((lane // 16) & step) != 0
                for k in range(8):
                    if k & step:
                        continue
                    a, b = pieces[k], pieces[k + step]
                    pieces[k] = jnp.where(upper, pltpu.roll(b, 16 * step, 1), a)
                    pieces[k + step] = jnp.where(upper, b, pltpu.roll(a, 128 - 16 * step, 1))
            for c in range(8):
                keep(pieces[c], grouped_ref, ((part * 8 + c) * rows + half * 8) * 16)


def project_kernel(
    rows,
    columns,
    scale,
    salt_ref,
    early_ref,
    grads_ref,
    *refs,
):
    out_ref, grouped_ref, staged_ref, partial_ref, signs_ref, sems = refs[-6:]
    devices = out_ref.shape[0]
    late = FEAT // TILE - EARLY

    def fetch(index):
        size = early_ref.shape[1] // SPLIT
        pieces = [(index, pl.ds(piece * size, size)) for piece in range(SPLIT)]
        return [
            pltpu.make_async_copy(early_ref.at[at], signs_ref.at[at], sems.at[index, piece])
            for piece, at in enumerate(pieces)
        ]

    def start(indices):
        for index in indices:
            for copy in fetch(index):
                copy.start()

    def wait(indices):
        for index in indices:
            for copy in fetch(index):
                copy.wait()

    start(range(min(EARLY, AHEAD)))

    def product(start, signs):
        updates = grouped_ref[:, start : start + signs.shape[0]]
        return jnp.dot(updates, signs, preferred_element_type=jnp.float32)

    def finish(tile, total):
        total = (total[:devices] + total[devices:]) * scale
        for part in range(TILE // 128):
            start = (tile * (TILE // 128) + part) * devices
            partial_ref[start : start + devices, :] = total[:, part * 128 : part * 128 + 128]

    if len(refs) > 6:
        regroup(rows, grads_ref, *refs[:2], grouped_ref, staged_ref)
    else:
        keep(grads_ref[...], grouped_ref, 0)

    salt = salt_ref[0]
    heights = row_heights(salt, rows)
    batches = [range(at, min(EARLY, at + AHEAD)) for at in range(0, EARLY, AHEAD)]
    fetched, ready = 0, []
    blocks = columns // 16
    depth = rows * 16
    half = max(blocks // 2, 1)
    group = math.gcd(half, GROUP)

    def take():
        nonlocal fetched
        wait(batches[fetched])
        ready.extend(batches[fetched])
        fetched += 1
        if fetched < len(batches):
            start(batches[fetched])

    for step in range(late * (blocks // half)):
        if fetched < len(batches) and step >= FIRST + fetched * EACH:
            take()
        tile, first = divmod(step * half, blocks)
        stored = ready.pop(0) if ready else None
        if first == 0:
            lanes = lane_terms(salt, tile)
            made = 0.0
        other = 0.0
        for block in range(first, first + half, group):
            if stored is not None:
                share = signs_ref.shape[1] // (half // group)
                begin = (block - first) // group * share
                other += product(begin, signs_ref[stored, begin : begin + share, :])
            signs = [
                block_signs(salt, columns, lanes, heights, block + member)
                for member in range(group)
            ]
            made += product(block * depth, jnp.concatenate(signs, 0))
        if first + half == blocks:
            finish(tile, made)
        if stored is not None:
            finish(late + stored, other)
    while ready or fetched < len(batches):
        if not ready:
            take()
        stored = ready.pop(0)
        finish(late + stored, product(0, signs_ref[stored]))

    for device in range(devices):
        out_ref[device] = partial_ref[
            pl.ds(device, FEAT // 128, stride=devices), :
        ].astype(jnp.bfloat16)


def project(salt, grads, first, second, early, scale):
    m, rows, columns = grads.shape
    vmem = pl.BlockSpec(memory_space=pltpu.VMEM)
    if rows % 16 == 0 and columns % 128 == 0:
        first, second = first.reshape(-1, 128), second.reshape(-1, 128)
        operands = (grads.reshape(m * rows, columns), first, second)
    else:

        def share(moment):
            start = lax.axis_index("wide") * columns
            return lax.dynamic_slice_in_dim(moment.reshape(rows, -1), start, columns, 1)

        flat = adam_scale(grads.astype(jnp.float32), share(first)[None], share(second)[None])
        flat = flat.reshape(m, rows, columns // 16, 16).transpose(0, 2, 1, 3)
        operands = (flat.reshape(m, rows * columns),)
    return pl.pallas_call(
        functools.partial(project_kernel, rows, columns, scale),
        out_shape=jax.ShapeDtypeStruct((m, FEAT // 128, 128), jnp.bfloat16),
        in_specs=[
            pl.BlockSpec(memory_space=pltpu.SMEM),
            pl.BlockSpec(memory_space=pl.ANY),
        ]
        + [vmem] * len(operands),
        out_specs=vmem,
        scratch_shapes=[
            pltpu.VMEM((2 * m, rows * columns), jnp.bfloat16),
            pltpu.VMEM((m * rows, 128), jnp.float32),
            pltpu.VMEM((FEAT // 128 * m, 128), jnp.float32),
            pltpu.VMEM((EARLY, rows * columns, TILE), SIGN),
            pltpu.SemaphoreType.DMA((EARLY, SPLIT)),
        ],
        compiler_params=pltpu.CompilerParams(vmem_limit_bytes=44 << 20),
        name="project",
    )(salt, early, *operands)


def body(
    groups,
    holders,
    acts,
    cotangent,
    down_matrix,
    up_matrix,
    adam_first_moment,
    adam_second_moment,
    lengths,
    sign_hash_salt,
):
    rank, inputs = down_matrix.shape
    rank_rows = 2 * rank
    rows, columns = rank_rows // holders, inputs // groups
    params = rank_rows * inputs
    slabs = sequence_grads(groups, holders, acts, cotangent, down_matrix, up_matrix, lengths)
    early = early_signs(sign_hash_salt, rows, columns, slabs)
    grads = lax.all_to_all(slabs, AXES, 0, 0, tiled=True)
    partial = project(
        sign_hash_salt, grads, adam_first_moment, adam_second_moment, early, params**-0.5
    )
    parts = lax.all_to_all(partial, AXES, 0, 0, tiled=True)
    return jnp.sum(parts.astype(jnp.float32), axis=0).reshape(1, FEAT)


def solution(mesh):
    groups, holders = mesh.shape["wide"], mesh.shape["narrow"]
    placed = (
        P(AXES, None, None),
        P(AXES, None, None),
        P(),
        P(),
        P("narrow"),
        P("narrow"),
        P(AXES),
        P(),
    )
    return jax.shard_map(
        functools.partial(body, groups, holders),
        mesh=mesh,
        in_specs=placed,
        out_specs=P(AXES, None),
        check_vma=False,
    )
```

```python
import functools
import math

import jax
import jax.numpy as jnp
import numpy as np
from jax import lax
from jax.experimental import pallas as pl
from jax.experimental.pallas import tpu as pltpu
from jax.sharding import PartitionSpec as P

FEAT = 4096
MUL_A = 747796405
MUL_B = 277803737
AXES = ("wide", "narrow")
COLUMN_BITS = 11
LOW = (1 << COLUMN_BITS) - 1
TILE = 512
GROUP = 2
SPLIT = 8
FIRST, EACH = 5, 9
NEXT = 3
AHEAD = 3
EARLY = 5
I16 = jnp.int16
I32 = jnp.int32
SIGN = jnp.float8_e4m3fn


def short(value):
    value &= 0xFFFF
    return np.int16(value - 65536 if value >= 32768 else value)


def grads_kernel(holders, length_ref, acts_ref, cot_ref, down_ref, up_ref, grads_ref):
    groups, (rows, columns) = grads_ref.shape[0] // holders, grads_ref.shape[1:]
    acts = acts_ref[...]
    slots = lax.broadcasted_iota(I32, cot_ref.shape, 0)
    masked = jnp.where(slots < length_ref[0], cot_ref[...].astype(jnp.float32), 0.0)
    masked = masked.astype(jnp.bfloat16)
    last = (((1,), (1,)), ((), ()))
    first = (((0,), (0,)), ((), ()))
    hidden = lax.dot_general(acts, down_ref[...], last, preferred_element_type=jnp.float32)
    inner = lax.dot_general(masked, up_ref[...], last, preferred_element_type=jnp.float32)
    for half, (left, right) in enumerate(((inner, acts), (hidden, masked))):
        grads = lax.dot_general(
            left.astype(jnp.bfloat16), right, first, preferred_element_type=jnp.float32
        )
        for holder in range(holders // 2):
            for group in range(groups):
                grads_ref[group * holders + half * (holders // 2) + holder] = grads[
                    holder * rows : (holder + 1) * rows, group * columns : (group + 1) * columns
                ].astype(jnp.bfloat16)


def sequence_grads(groups, holders, acts, cotangent, down_matrix, up_matrix, lengths):
    rank, inputs = down_matrix.shape
    vmem = pl.BlockSpec(memory_space=pltpu.VMEM)
    slabs = (groups * holders, 2 * rank // holders, inputs // groups)
    return pl.pallas_call(
        functools.partial(grads_kernel, holders),
        out_shape=jax.ShapeDtypeStruct(slabs, jnp.bfloat16),
        in_specs=[pl.BlockSpec(memory_space=pltpu.SMEM)] + [vmem] * 4,
        out_specs=vmem,
        name="grads",
    )(lengths, acts[0], cotangent[0], down_matrix, up_matrix.T)


def position():
    return lax.axis_index("wide"), lax.axis_index("narrow")


def lane_terms(salt, tile):
    feature = lax.broadcasted_iota(I32, (8, TILE), 1) + tile * TILE
    product = (feature ^ (salt & (FEAT - 1))) * MUL_A + 1
    low = product & (FEAT - 1)
    high = lax.shift_right_logical(product, 12)

    def packed(x):
        return jnp.concatenate([x, x], 0).astype(I16)

    return (
        packed(high & LOW),
        packed(((high >> COLUMN_BITS) & 511) + 256),
        packed(low >> 8),
        packed((low & 255) << 3),
    )


def column_terms(salt, first, lanes):
    lane_low, lane_high, lane_top, lane_byte = lanes
    column = lax.broadcasted_iota(I32, (16, 128), 0) + first
    product = ((column ^ ((salt >> 12) & LOW)) * MUL_A) & 0xFFFFF
    row_low = (product & LOW).astype(I16)
    row_high = (product >> COLUMN_BITS).astype(I16)
    wide = (1, TILE // 128)
    row_low, row_high = jnp.tile(row_low, wide), jnp.tile(row_high, wide)
    total = row_low + lane_low
    height = row_high + lane_high + lax.shift_right_logical(total, I16(COLUMN_BITS))
    mixed = total * I16(16) + lane_top
    byte8 = (total ^ lane_byte) & I16(0x7F8)
    byte = lax.shift_right_logical(byte8, I16(3))
    tail = byte * I16(MUL_B & 255)
    carry = byte8 * short(MUL_B >> 8) + lax.shift_right_logical(tail, I16(5))
    carry = carry + ((tail * I16(256)) & I16(-32768))
    return height, mixed, carry


def row_heights(salt, rows):
    first = position()[1] * rows
    heights = [(((first + k) ^ (salt >> (12 + COLUMN_BITS))) * MUL_A) & 511 for k in range(rows)]
    return [jnp.full((16, TILE), h, I32).astype(I16) for h in heights]


def block_signs(salt, columns, lanes, heights, block):
    height, mixed, carry = column_terms(salt, position()[0] * columns + block * 16, lanes)
    values = []
    for row in heights:
        value = (((height + row) & I16(511)) - I16(256)) ^ mixed
        values.append(value * short(8 * MUL_B) + carry)
    return jnp.where(jnp.concatenate(values, 0) < 0, SIGN(-1), SIGN(1))


def signs_kernel(rows, columns, salt_ref, after_ref, out_ref):
    del after_ref
    salt = salt_ref[0]
    lanes = lane_terms(salt, pl.program_id(0) + FEAT // TILE - EARLY)
    heights = row_heights(salt, rows)
    depth = 16 * rows
    blocks = out_ref.shape[1] // depth
    first = pl.program_id(1) * blocks

    def store(block, _):
        here = pl.ds(pl.multiple_of(block * depth, depth), depth)
        out_ref[0, here, :] = block_signs(salt, columns, lanes, heights, first + block)
        return 0

    lax.fori_loop(0, blocks, store, 0, unroll=2)


def early_signs(salt, rows, columns, after):
    size = rows * columns
    return pl.pallas_call(
        functools.partial(signs_kernel, rows, columns),
        out_shape=jax.ShapeDtypeStruct((EARLY, size, TILE), SIGN),
        grid_spec=pltpu.PrefetchScalarGridSpec(
            num_scalar_prefetch=1,
            grid=(EARLY, 2),
            in_specs=[pl.BlockSpec(memory_space=pl.ANY)],
            out_specs=pl.BlockSpec((1, size // 2, TILE), lambda t, h, i: (t, h, 0)),
        ),
        cost_estimate=pl.CostEstimate(
            flops=EARLY * size * TILE * 256, bytes_accessed=0, transcendentals=0
        ),
        name="early_signs",
    )(salt, after)


def adam_scale(grads, first, second):
    moment_one = 0.9 * first + 0.1 * grads
    moment_two = 0.999 * second + 0.001 * grads * grads
    return moment_one / (jnp.sqrt(moment_two) + 1e-08)


def keep(updates, grouped_ref, start):
    devices, size = updates.shape
    high = updates.astype(jnp.bfloat16)
    grouped_ref[:devices, start : start + size] = high
    low = updates - high.astype(jnp.float32)
    grouped_ref[devices:, start : start + size] = low.astype(jnp.bfloat16)


def regroup(rows, grads_ref, first_ref, second_ref, grouped_ref, staged_ref):
    columns = grads_ref.shape[1]
    devices = grads_ref.shape[0] // rows
    stride = first_ref.shape[0] // rows
    lane = lax.broadcasted_iota(I32, (devices, 128), 1)
    for part in range(columns // 128):
        lanes = slice(part * 128, part * 128 + 128)
        share = pl.ds(position()[0] * (columns // 128) + part, rows, stride=stride)
        first, second = first_ref[share, :], second_ref[share, :]
        for device in range(devices):
            here = slice(device * rows, (device + 1) * rows)
            grads = grads_ref[here, lanes].astype(jnp.float32)
            staged_ref[here, :] = adam_scale(grads, first, second)
        for half in range(rows // 8):
            pieces = [
                staged_ref[pl.ds(half * 8 + k, devices, stride=rows), :] for k in range(8)
            ]
            for step in (4, 2, 1):
                upper = ((lane // 16) & step) != 0
                for k in range(8):
                    if k & step:
                        continue
                    a, b = pieces[k], pieces[k + step]
                    pieces[k] = jnp.where(upper, pltpu.roll(b, 16 * step, 1), a)
                    pieces[k + step] = jnp.where(upper, b, pltpu.roll(a, 128 - 16 * step, 1))
            for c in range(8):
                keep(pieces[c], grouped_ref, ((part * 8 + c) * rows + half * 8) * 16)


def project_kernel(
    rows,
    columns,
    scale,
    salt_ref,
    early_ref,
    grads_ref,
    *refs,
):
    out_ref, grouped_ref, staged_ref, partial_ref, signs_ref, sems = refs[-6:]
    devices = out_ref.shape[0]
    late = FEAT // TILE - EARLY

    def fetch(index):
        size = early_ref.shape[1] // SPLIT
        pieces = [(index, pl.ds(piece * size, size)) for piece in range(SPLIT)]
        return [
            pltpu.make_async_copy(early_ref.at[at], signs_ref.at[at], sems.at[index, piece])
            for piece, at in enumerate(pieces)
        ]

    def start(indices):
        for index in indices:
            for copy in fetch(index):
                copy.start()

    def wait(indices):
        for index in indices:
            for copy in fetch(index):
                copy.wait()

    start(range(min(EARLY, AHEAD)))

    def product(start, signs):
        updates = grouped_ref[:, start : start + signs.shape[0]]
        return jnp.dot(updates, signs, preferred_element_type=jnp.float32)

    def finish(tile, total):
        total = (total[:devices] + total[devices:]) * scale
        for part in range(TILE // 128):
            start = (tile * (TILE // 128) + part) * devices
            partial_ref[start : start + devices, :] = total[:, part * 128 : part * 128 + 128]

    if len(refs) > 6:
        regroup(rows, grads_ref, *refs[:2], grouped_ref, staged_ref)
    else:
        keep(grads_ref[...], grouped_ref, 0)

    salt = salt_ref[0]
    heights = row_heights(salt, rows)
    batches = [range(at, min(EARLY, at + AHEAD)) for at in range(0, EARLY, AHEAD)]
    fetched, started, ready = 0, 1, []
    blocks = columns // 16
    depth = rows * 16
    half = max(blocks // 2, 1)
    group = math.gcd(half, GROUP)

    def begin_next(count):
        nonlocal started
        while started < min(count, len(batches)):
            start(batches[started])
            started += 1

    def take():
        nonlocal fetched
        begin_next(fetched + 1)
        wait(batches[fetched])
        ready.extend(batches[fetched])
        fetched += 1

    for step in range(late * (blocks // half)):
        if step == NEXT:
            begin_next(2)
        if fetched < len(batches) and step >= FIRST + fetched * EACH:
            take()
        tile, first = divmod(step * half, blocks)
        stored = ready.pop(0) if ready else None
        if first == 0:
            lanes = lane_terms(salt, tile)
            made = 0.0
        other = 0.0
        for block in range(first, first + half, group):
            if stored is not None:
                share = signs_ref.shape[1] // (half // group)
                begin = (block - first) // group * share
                other += product(begin, signs_ref[stored, begin : begin + share, :])
            signs = [
                block_signs(salt, columns, lanes, heights, block + member)
                for member in range(group)
            ]
            made += product(block * depth, jnp.concatenate(signs, 0))
        if first + half == blocks:
            finish(tile, made)
        if stored is not None:
            finish(late + stored, other)
    while ready or fetched < len(batches):
        if not ready:
            take()
        stored = ready.pop(0)
        finish(late + stored, product(0, signs_ref[stored]))

    for device in range(devices):
        out_ref[device] = partial_ref[
            pl.ds(device, FEAT // 128, stride=devices), :
        ].astype(jnp.bfloat16)


def project(salt, grads, first, second, early, scale):
    m, rows, columns = grads.shape
    vmem = pl.BlockSpec(memory_space=pltpu.VMEM)
    if rows % 16 == 0 and columns % 128 == 0:
        first, second = first.reshape(-1, 128), second.reshape(-1, 128)
        operands = (grads.reshape(m * rows, columns), first, second)
    else:

        def share(moment):
            start = lax.axis_index("wide") * columns
            return lax.dynamic_slice_in_dim(moment.reshape(rows, -1), start, columns, 1)

        flat = adam_scale(grads.astype(jnp.float32), share(first)[None], share(second)[None])
        flat = flat.reshape(m, rows, columns // 16, 16).transpose(0, 2, 1, 3)
        operands = (flat.reshape(m, rows * columns),)
    return pl.pallas_call(
        functools.partial(project_kernel, rows, columns, scale),
        out_shape=jax.ShapeDtypeStruct((m, FEAT // 128, 128), jnp.bfloat16),
        in_specs=[
            pl.BlockSpec(memory_space=pltpu.SMEM),
            pl.BlockSpec(memory_space=pl.ANY),
        ]
        + [vmem] * len(operands),
        out_specs=vmem,
        scratch_shapes=[
            pltpu.VMEM((2 * m, rows * columns), jnp.bfloat16),
            pltpu.VMEM((m * rows, 128), jnp.float32),
            pltpu.VMEM((FEAT // 128 * m, 128), jnp.float32),
            pltpu.VMEM((EARLY, rows * columns, TILE), SIGN),
            pltpu.SemaphoreType.DMA((EARLY, SPLIT)),
        ],
        compiler_params=pltpu.CompilerParams(vmem_limit_bytes=44 << 20),
        name="project",
    )(salt, early, *operands)


def body(
    groups,
    holders,
    acts,
    cotangent,
    down_matrix,
    up_matrix,
    adam_first_moment,
    adam_second_moment,
    lengths,
    sign_hash_salt,
):
    rank, inputs = down_matrix.shape
    rank_rows = 2 * rank
    rows, columns = rank_rows // holders, inputs // groups
    params = rank_rows * inputs
    slabs = sequence_grads(groups, holders, acts, cotangent, down_matrix, up_matrix, lengths)
    early = early_signs(sign_hash_salt, rows, columns, slabs)
    grads = lax.all_to_all(slabs, AXES, 0, 0, tiled=True)
    partial = project(
        sign_hash_salt, grads, adam_first_moment, adam_second_moment, early, params**-0.5
    )
    parts = lax.all_to_all(partial, AXES, 0, 0, tiled=True)
    return jnp.sum(parts.astype(jnp.float32), axis=0).reshape(1, FEAT)


def solution(mesh):
    groups, holders = mesh.shape["wide"], mesh.shape["narrow"]
    placed = (
        P(AXES, None, None),
        P(AXES, None, None),
        P(),
        P(),
        P("narrow"),
        P("narrow"),
        P(AXES),
        P(),
    )
    return jax.shard_map(
        functools.partial(body, groups, holders),
        mesh=mesh,
        in_specs=placed,
        out_specs=P(AXES, None),
        check_vma=False,
    )
```

```python
import functools
import math

import jax
import jax.numpy as jnp
import numpy as np
from jax import lax
from jax.experimental import pallas as pl
from jax.experimental.pallas import tpu as pltpu
from jax.sharding import PartitionSpec as P

FEAT = 4096
MUL_A = 747796405
MUL_B = 277803737
AXES = ("wide", "narrow")
COLUMN_BITS = 11
LOW = (1 << COLUMN_BITS) - 1
TILE = 512
GROUP = 2
SPLIT = 8
FIRST, EACH = 5, 9
NEXT = 3
AHEAD = 3
EARLY = 5
I16 = jnp.int16
I32 = jnp.int32
SIGN = jnp.float8_e4m3fn


def short(value):
    value &= 0xFFFF
    return np.int16(value - 65536 if value >= 32768 else value)


def grads_kernel(holders, length_ref, acts_ref, cot_ref, down_ref, up_ref, grads_ref):
    groups, (rows, columns) = grads_ref.shape[0] // holders, grads_ref.shape[1:]
    acts = acts_ref[...]
    slots = lax.broadcasted_iota(I32, cot_ref.shape, 0)
    masked = jnp.where(slots < length_ref[0], cot_ref[...].astype(jnp.float32), 0.0)
    masked = masked.astype(jnp.bfloat16)
    last = (((1,), (1,)), ((), ()))
    first = (((0,), (0,)), ((), ()))
    hidden = lax.dot_general(acts, down_ref[...], last, preferred_element_type=jnp.float32)
    inner = lax.dot_general(masked, up_ref[...], last, preferred_element_type=jnp.float32)
    for half, (left, right) in enumerate(((inner, acts), (hidden, masked))):
        grads = lax.dot_general(
            left.astype(jnp.bfloat16), right, first, preferred_element_type=jnp.float32
        )
        for holder in range(holders // 2):
            for group in range(groups):
                grads_ref[group * holders + half * (holders // 2) + holder] = grads[
                    holder * rows : (holder + 1) * rows, group * columns : (group + 1) * columns
                ].astype(jnp.bfloat16)


def sequence_grads(groups, holders, acts, cotangent, down_matrix, up_matrix, lengths):
    rank, inputs = down_matrix.shape
    vmem = pl.BlockSpec(memory_space=pltpu.VMEM)
    slabs = (groups * holders, 2 * rank // holders, inputs // groups)
    return pl.pallas_call(
        functools.partial(grads_kernel, holders),
        out_shape=jax.ShapeDtypeStruct(slabs, jnp.bfloat16),
        in_specs=[pl.BlockSpec(memory_space=pltpu.SMEM)] + [vmem] * 4,
        out_specs=vmem,
        name="grads",
    )(lengths, acts[0], cotangent[0], down_matrix, up_matrix.T)


def position():
    return lax.axis_index("wide"), lax.axis_index("narrow")


def lane_terms(salt, tile):
    feature = lax.broadcasted_iota(I32, (8, TILE), 1) + tile * TILE
    product = (feature ^ (salt & (FEAT - 1))) * MUL_A + 1
    low = product & (FEAT - 1)
    high = lax.shift_right_logical(product, 12)

    def packed(x):
        return jnp.concatenate([x, x], 0).astype(I16)

    return (
        packed(high & LOW),
        packed(((high >> COLUMN_BITS) & 511) + 256),
        packed(low >> 8),
        packed((low & 255) << 3),
    )


def column_terms(salt, first, lanes):
    lane_low, lane_high, lane_top, lane_byte = lanes
    column = lax.broadcasted_iota(I32, (16, 128), 0) + first
    product = ((column ^ ((salt >> 12) & LOW)) * MUL_A) & 0xFFFFF
    row_low = (product & LOW).astype(I16)
    row_high = (product >> COLUMN_BITS).astype(I16)
    wide = (1, TILE // 128)
    row_low, row_high = jnp.tile(row_low, wide), jnp.tile(row_high, wide)
    total = row_low + lane_low
    height = row_high + lane_high + lax.shift_right_logical(total, I16(COLUMN_BITS))
    mixed = total * I16(16) + lane_top
    byte8 = (total ^ lane_byte) & I16(0x7F8)
    byte = lax.shift_right_logical(byte8, I16(3))
    tail = byte * I16(MUL_B & 255)
    carry = byte8 * short(MUL_B >> 8) + lax.shift_right_logical(tail, I16(5))
    carry = carry + ((tail * I16(256)) & I16(-32768))
    return height, mixed, carry


def row_heights(salt, rows):
    first = position()[1] * rows
    heights = [(((first + k) ^ (salt >> (12 + COLUMN_BITS))) * MUL_A) & 511 for k in range(rows)]
    return [jnp.full((16, TILE), h, I32).astype(I16) for h in heights]


def block_signs(salt, columns, lanes, heights, block):
    height, mixed, carry = column_terms(salt, position()[0] * columns + block * 16, lanes)
    values = []
    for row in heights:
        value = (((height + row) & I16(511)) - I16(256)) ^ mixed
        values.append(value * short(8 * MUL_B) + carry)
    return jnp.where(jnp.concatenate(values, 0) < 0, SIGN(-1), SIGN(1))


def signs_kernel(rows, columns, salt_ref, after_ref, out_ref):
    del after_ref
    salt = salt_ref[0]
    lanes = lane_terms(salt, pl.program_id(0) + FEAT // TILE - EARLY)
    heights = row_heights(salt, rows)
    depth = 16 * rows
    blocks = out_ref.shape[1] // depth
    first = pl.program_id(1) * blocks

    def store(block, _):
        here = pl.ds(pl.multiple_of(block * depth, depth), depth)
        out_ref[0, here, :] = block_signs(salt, columns, lanes, heights, first + block)
        return 0

    lax.fori_loop(0, blocks, store, 0, unroll=2)


def early_signs(salt, rows, columns, after):
    size = rows * columns
    return pl.pallas_call(
        functools.partial(signs_kernel, rows, columns),
        out_shape=jax.ShapeDtypeStruct((EARLY, size, TILE), SIGN),
        grid_spec=pltpu.PrefetchScalarGridSpec(
            num_scalar_prefetch=1,
            grid=(EARLY, 4),
            in_specs=[pl.BlockSpec(memory_space=pl.ANY)],
            out_specs=pl.BlockSpec((1, size // 4, TILE), lambda t, h, i: (t, h, 0)),
        ),
        cost_estimate=pl.CostEstimate(
            flops=EARLY * size * TILE * 256, bytes_accessed=0, transcendentals=0
        ),
        name="early_signs",
    )(salt, after)


def adam_scale(grads, first, second):
    moment_one = 0.9 * first + 0.1 * grads
    moment_two = 0.999 * second + 0.001 * grads * grads
    return moment_one / (jnp.sqrt(moment_two) + 1e-08)


def keep(updates, grouped_ref, start):
    devices, size = updates.shape
    high = updates.astype(jnp.bfloat16)
    grouped_ref[:devices, start : start + size] = high
    low = updates - high.astype(jnp.float32)
    grouped_ref[devices:, start : start + size] = low.astype(jnp.bfloat16)


def regroup(rows, grads_ref, first_ref, second_ref, grouped_ref, staged_ref):
    columns = grads_ref.shape[1]
    devices = grads_ref.shape[0] // rows
    stride = first_ref.shape[0] // rows
    lane = lax.broadcasted_iota(I32, (devices, 128), 1)
    for part in range(columns // 128):
        lanes = slice(part * 128, part * 128 + 128)
        share = pl.ds(position()[0] * (columns // 128) + part, rows, stride=stride)
        first, second = first_ref[share, :], second_ref[share, :]
        for device in range(devices):
            here = slice(device * rows, (device + 1) * rows)
            grads = grads_ref[here, lanes].astype(jnp.float32)
            staged_ref[here, :] = adam_scale(grads, first, second)
        for half in range(rows // 8):
            pieces = [
                staged_ref[pl.ds(half * 8 + k, devices, stride=rows), :] for k in range(8)
            ]
            for step in (4, 2, 1):
                upper = ((lane // 16) & step) != 0
                for k in range(8):
                    if k & step:
                        continue
                    a, b = pieces[k], pieces[k + step]
                    pieces[k] = jnp.where(upper, pltpu.roll(b, 16 * step, 1), a)
                    pieces[k + step] = jnp.where(upper, b, pltpu.roll(a, 128 - 16 * step, 1))
            for c in range(8):
                keep(pieces[c], grouped_ref, ((part * 8 + c) * rows + half * 8) * 16)


def project_kernel(
    rows,
    columns,
    scale,
    salt_ref,
    early_ref,
    grads_ref,
    *refs,
):
    out_ref, grouped_ref, staged_ref, partial_ref, signs_ref, sems = refs[-6:]
    devices = out_ref.shape[0]
    late = FEAT // TILE - EARLY

    def fetch(index):
        size = early_ref.shape[1] // SPLIT
        pieces = [(index, pl.ds(piece * size, size)) for piece in range(SPLIT)]
        return [
            pltpu.make_async_copy(early_ref.at[at], signs_ref.at[at], sems.at[index, piece])
            for piece, at in enumerate(pieces)
        ]

    def start(indices):
        for index in indices:
            for copy in fetch(index):
                copy.start()

    def wait(indices):
        for index in indices:
            for copy in fetch(index):
                copy.wait()

    start(range(min(EARLY, AHEAD)))

    def product(start, signs):
        updates = grouped_ref[:, start : start + signs.shape[0]]
        return jnp.dot(updates, signs, preferred_element_type=jnp.float32)

    def finish(tile, total):
        total = (total[:devices] + total[devices:]) * scale
        for part in range(TILE // 128):
            start = (tile * (TILE // 128) + part) * devices
            partial_ref[start : start + devices, :] = total[:, part * 128 : part * 128 + 128]

    if len(refs) > 6:
        regroup(rows, grads_ref, *refs[:2], grouped_ref, staged_ref)
    else:
        keep(grads_ref[...], grouped_ref, 0)

    salt = salt_ref[0]
    heights = row_heights(salt, rows)
    batches = [range(at, min(EARLY, at + AHEAD)) for at in range(0, EARLY, AHEAD)]
    fetched, started, ready = 0, 1, []
    blocks = columns // 16
    depth = rows * 16
    half = max(blocks // 2, 1)
    group = math.gcd(half, GROUP)

    def begin_next(count):
        nonlocal started
        while started < min(count, len(batches)):
            start(batches[started])
            started += 1

    def take():
        nonlocal fetched
        begin_next(fetched + 1)
        wait(batches[fetched])
        ready.extend(batches[fetched])
        fetched += 1

    for step in range(late * (blocks // half)):
        if step == NEXT:
            begin_next(2)
        if fetched < len(batches) and step >= FIRST + fetched * EACH:
            take()
        tile, first = divmod(step * half, blocks)
        stored = ready.pop(0) if ready else None
        if first == 0:
            lanes = lane_terms(salt, tile)
            made = 0.0
        other = 0.0
        for block in range(first, first + half, group):
            if stored is not None:
                share = signs_ref.shape[1] // (half // group)
                begin = (block - first) // group * share
                other += product(begin, signs_ref[stored, begin : begin + share, :])
            signs = [
                block_signs(salt, columns, lanes, heights, block + member)
                for member in range(group)
            ]
            made += product(block * depth, jnp.concatenate(signs, 0))
        if first + half == blocks:
            finish(tile, made)
        if stored is not None:
            finish(late + stored, other)
    while ready or fetched < len(batches):
        if not ready:
            take()
        stored = ready.pop(0)
        finish(late + stored, product(0, signs_ref[stored]))

    for device in range(devices):
        out_ref[device] = partial_ref[
            pl.ds(device, FEAT // 128, stride=devices), :
        ].astype(jnp.bfloat16)


def project(salt, grads, first, second, early, scale):
    m, rows, columns = grads.shape
    vmem = pl.BlockSpec(memory_space=pltpu.VMEM)
    if rows % 16 == 0 and columns % 128 == 0:
        first, second = first.reshape(-1, 128), second.reshape(-1, 128)
        operands = (grads.reshape(m * rows, columns), first, second)
    else:

        def share(moment):
            start = lax.axis_index("wide") * columns
            return lax.dynamic_slice_in_dim(moment.reshape(rows, -1), start, columns, 1)

        flat = adam_scale(grads.astype(jnp.float32), share(first)[None], share(second)[None])
        flat = flat.reshape(m, rows, columns // 16, 16).transpose(0, 2, 1, 3)
        operands = (flat.reshape(m, rows * columns),)
    return pl.pallas_call(
        functools.partial(project_kernel, rows, columns, scale),
        out_shape=jax.ShapeDtypeStruct((m, FEAT // 128, 128), jnp.bfloat16),
        in_specs=[
            pl.BlockSpec(memory_space=pltpu.SMEM),
            pl.BlockSpec(memory_space=pl.ANY),
        ]
        + [vmem] * len(operands),
        out_specs=vmem,
        scratch_shapes=[
            pltpu.VMEM((2 * m, rows * columns), jnp.bfloat16),
            pltpu.VMEM((m * rows, 128), jnp.float32),
            pltpu.VMEM((FEAT // 128 * m, 128), jnp.float32),
            pltpu.VMEM((EARLY, rows * columns, TILE), SIGN),
            pltpu.SemaphoreType.DMA((EARLY, SPLIT)),
        ],
        compiler_params=pltpu.CompilerParams(vmem_limit_bytes=44 << 20),
        name="project",
    )(salt, early, *operands)


def body(
    groups,
    holders,
    acts,
    cotangent,
    down_matrix,
    up_matrix,
    adam_first_moment,
    adam_second_moment,
    lengths,
    sign_hash_salt,
):
    rank, inputs = down_matrix.shape
    rank_rows = 2 * rank
    rows, columns = rank_rows // holders, inputs // groups
    params = rank_rows * inputs
    slabs = sequence_grads(groups, holders, acts, cotangent, down_matrix, up_matrix, lengths)
    early = early_signs(sign_hash_salt, rows, columns, slabs)
    grads = lax.all_to_all(slabs, AXES, 0, 0, tiled=True)
    partial = project(
        sign_hash_salt, grads, adam_first_moment, adam_second_moment, early, params**-0.5
    )
    parts = lax.all_to_all(partial, AXES, 0, 0, tiled=True)
    return jnp.sum(parts.astype(jnp.float32), axis=0).reshape(1, FEAT)


def solution(mesh):
    groups, holders = mesh.shape["wide"], mesh.shape["narrow"]
    placed = (
        P(AXES, None, None),
        P(AXES, None, None),
        P(),
        P(),
        P("narrow"),
        P("narrow"),
        P(AXES),
        P(),
    )
    return jax.shard_map(
        functools.partial(body, groups, holders),
        mesh=mesh,
        in_specs=placed,
        out_specs=P(AXES, None),
        check_vma=False,
    )
```
